32 devices in a mesh: seq: 4 (over z), dp: 8 (over y, x, core).
Axes of the slice: x: 2, y: 2, z: 4, core: 2. Of those that a mesh axis runs over, the one named last changes fastest.
Arguments:
- tokens: bfloat16 [2, 8, 1024, 2048], P(None, 'dp', 'seq'), may hold values from -6 to 6
- cotangent: bfloat16 [2, 8, 1024, 2048], P(None, 'dp', 'seq'), may hold values from -6 to 6
- doc_lengths: int32 [2, 8, 4], P(None, 'dp'), may hold values from 1 to 512, 1024 in all within a row
- pad_lengths: int32 [2, 8], P(None, 'dp'), may hold values from 0 to 256
- attn_gain: bfloat16 [2048], P(('seq', 'dp')), may hold values from 0.5 to 1.5
- query_down: bfloat16 [2048, 1024], P(('seq', 'dp')), may hold values from -0.125 to 0.125
- query_gain: bfloat16 [1024], P(('seq', 'dp')), may hold values from 0.5 to 1.5
- query_up: bfloat16 [1024, 4096], P(None, ('seq', 'dp')), may hold values from -0.1875 to 0.1875
- key_weight: bfloat16 [2048, 256], P(('seq', 'dp')), may hold values from -0.25 to 0.25
- value_weight: bfloat16 [2048, 256], P(('seq', 'dp')), may hold values from -0.125 to 0.125
- out_weight: bfloat16 [4096, 2048], P(('seq', 'dp')), may hold values from -0.5 to 0.5
- ffn_gain: bfloat16 [2048], P(('seq', 'dp')), may hold values from 0.5 to 1.5
- gate_weight: bfloat16 [2048, 5632], P(None, ('seq', 'dp')), may hold values from -0.125 to 0.125
- up_weight: bfloat16 [2048, 5632], P(None, ('seq', 'dp')), may hold values from -0.125 to 0.125
- down_weight: bfloat16 [5632, 2048], P(('seq', 'dp')), may hold values from -0.078125 to 0.078125
Outputs:
- layer_out: bfloat16 [2, 8, 1024, 2048], P(None, 'dp', 'seq')
- tokens_grad: bfloat16 [2, 8, 1024, 2048], P(None, 'dp', 'seq')
- attn_gain_grad: float32 [2048], P(('seq', 'dp'))
- query_down_grad: float32 [2048, 1024], P(('seq', 'dp'))
- query_gain_grad: float32 [1024], P(('seq', 'dp'))
- query_up_grad: float32 [1024, 4096], P(None, ('seq', 'dp'))
- key_weight_grad: float32 [2048, 256], P(('seq', 'dp'))
- value_weight_grad: float32 [2048, 256], P(('seq', 'dp'))
- out_weight_grad: float32 [4096, 2048], P(('seq', 'dp'))
- ffn_gain_grad: float32 [2048], P(('seq', 'dp'))
- gate_weight_grad: float32 [2048, 5632], P(None, ('seq', 'dp'))
- up_weight_grad: float32 [2048, 5632], P(None, ('seq', 'dp'))
- down_weight_grad: float32 [5632, 2048], P(('seq', 'dp'))
The draws below stay inside these ranges and needn't reach their ends.
Inputs may be any that keep to these rules, and one draw needn't show every extreme that they name: `doc_lengths`: each row's 4 document lengths sum to 1024 and the longest is exactly 512.
All inputs are finite; a program needn't handle non-finite values.
Results may differ from the reference program's by a relative error of at most 0.019.
Values may be sent and summed in bfloat16 or wider, within the bound.
No kernel may reach another device: no remote copies, remote signals or barrier semaphores. Data moves between devices by JAX's collectives and lax.ppermute only.
A program may use at most 320 MiB of HBM per device.

```python
import math
import jax
import jax.numpy as jnp
import numpy as np
from jax import lax

D = 2048
RANK = 1024
HEADS = 16
HEAD_DIM = 256
FF = 5632
MICRO = 2
NDOC = 4
ROW_LEN = 1024
ROWS = 8
MOST = 512
PAD_MAX = 256


def with_ends(entries, key, least, high):
    longest = entries.shape.index(max(entries.shape))
    spots = []
    for shift in (0, 1):
        where = [jax.random.randint(jax.random.fold_in(key, axis), (), 0, length) for axis, length in enumerate(entries.shape)]
        where[longest] = (where[longest] + shift) % entries.shape[longest]
        spots.append(tuple(where))
    return entries.at[spots[0]].set(least).at[spots[1]].set(high)


def shard_levels(stream_key, extent, cuts, low, high):
    def one(position, parts):
        draws = jax.random.uniform(jax.random.fold_in(jax.random.fold_in(stream_key, 6), position), (parts,), jnp.float32, low / len(cuts), high / len(cuts))
        return jnp.repeat(jnp.exp(draws), extent[position] // parts).reshape((-1,) + (1,) * (len(extent) - position - 1))

    factor_of = one(*cuts[0])
    for cut in cuts[1:]:
        factor_of = factor_of * one(*cut)
    return factor_of


def profile(amount, total, reach, skew):
    loads = [(1 << 20) // math.isqrt(standing ** skew) + 1 for standing in range(2, amount + 1)]
    spare, given = total - reach - (amount - 1), [1] * (amount - 1)
    while spare > 0:
        candidates = [i for i in range(amount - 1) if given[i] < reach]
        pool, budget = sum([loads[i] for i in candidates]), spare
        for i in candidates:
            more = min(reach - given[i], max(1, budget * loads[i] // pool), spare)
            given[i] = given[i] + more
            spare = spare - more
    return np.array([reach] + given)


def ragged(own_key, number_of, total, bound, skew):
    if number_of == 2:
        one = jax.random.randint(own_key, (), max(1, total - bound), min(bound, total - 1) + 1)
        return jnp.stack([one, total - one])
    tallies = jnp.asarray(profile(number_of, total, bound, skew), jnp.int32)
    couples = (number_of - 1) // 2
    giver, taker = tallies[1:1 + 2 * couples:2], tallies[2:2 + 2 * couples:2]
    room = jnp.minimum(giver - 1, bound - taker)
    passed = jax.random.randint(jax.random.fold_in(own_key, 1), (couples,), 0, 1 << 20) % (room + 1)
    tallies = tallies.at[1:1 + 2 * couples:2].set(giver - passed).at[2:2 + 2 * couples:2].set(taker + passed)
    return tallies[jax.random.permutation(jax.random.fold_in(own_key, 2), number_of)]


def bell_draw(rng, dims, scale, bound, shards=(), kind=jnp.bfloat16):
    level = shard_levels(rng, dims, shards, -0.22, 0.18) if shards else 1.0
    drawn = jax.random.normal(rng, dims, jnp.float32) * scale * level
    return jnp.minimum(jnp.maximum(drawn, -bound), bound).astype(kind)


def setup_inputs(seed: int = 0) -> dict:
    key_of = jax.random.split(jax.random.key(seed), 16)
    tokens = bell_draw(key_of[0], (MICRO, ROWS, ROW_LEN, D), 1.0, 6.0, ((1, 8), (2, 4)))
    cotangent = bell_draw(key_of[1], (MICRO, ROWS, ROW_LEN, D), 1.0, 6.0, ((1, 8), (2, 4)))
    doc_lengths = jax.vmap(lambda own: ragged(own, NDOC, ROW_LEN, MOST, 2))(jax.random.split(key_of[2], MICRO * ROWS)).reshape((MICRO, ROWS, NDOC)).astype(jnp.int32)
    pad_lengths = with_ends(jax.random.randint(key_of[3], (MICRO, ROWS), 0, PAD_MAX + 1), jax.random.fold_in(key_of[3], 1), 0, PAD_MAX).astype(jnp.int32)
    attn_gain = jnp.clip(1.0 + 0.1 * jax.random.normal(key_of[4], (D,), jnp.float32), 0.5, 1.5).astype(jnp.bfloat16)
    query_down = bell_draw(key_of[5], (D, RANK), D ** -0.5, 0.125, ((0, 32),))
    query_gain = jnp.clip(1.0 + 0.1 * jax.random.normal(key_of[6], (RANK,), jnp.float32), 0.5, 1.5).astype(jnp.bfloat16)
    query_up = bell_draw(key_of[7], (RANK, HEADS * HEAD_DIM), RANK ** -0.5, 0.1875, ((1, 32),))
    key_weight = bell_draw(key_of[8], (D, HEAD_DIM), (D // 4) ** -0.5, 0.25, ((0, 32),))
    value_weight = bell_draw(key_of[9], (D, HEAD_DIM), D ** -0.5, 0.125, ((0, 32),))
    out_weight = bell_draw(key_of[10], (HEADS * HEAD_DIM, D), (HEADS * HEAD_DIM // 32) ** -0.5, 0.5, ((0, 32),))
    ffn_gain = jnp.clip(1.0 + 0.1 * jax.random.normal(key_of[11], (D,), jnp.float32), 0.5, 1.5).astype(jnp.bfloat16)
    gate_weight = bell_draw(key_of[12], (D, FF), D ** -0.5, 0.125, ((1, 32),))
    up_weight = bell_draw(key_of[13], (D, FF), D ** -0.5, 0.125, ((1, 32),))
    down_weight = bell_draw(key_of[14], (FF, D), FF ** -0.5, 0.078125, ((0, 32),))
    return dict(tokens=tokens, cotangent=cotangent, doc_lengths=doc_lengths, pad_lengths=pad_lengths, attn_gain=attn_gain, query_down=query_down, query_gain=query_gain, query_up=query_up, key_weight=key_weight, value_weight=value_weight, out_weight=out_weight, ffn_gain=ffn_gain, gate_weight=gate_weight, up_weight=up_weight, down_weight=down_weight)


EPSILON = 1e-05
THETA_BASE = 10000.0
NEG_FILL = -1e+30

@jax.custom_vjp
def low(v):
    return lax.optimization_barrier(v.astype(jnp.bfloat16)).astype(jnp.float32)

@jax.custom_vjp
def low_back(v):
    return v

def low_keep(v):
    return (low(v), None)

def low_pass(kept, grad):
    return (grad,)

def back_keep(v):
    return (v, None)

def back_low(kept, grad):
    return (low(grad),)
low.defvjp(low_keep, low_pass)
low_back.defvjp(back_keep, back_low)

def inv_norm(values):
    return lax.rsqrt(lax.optimization_barrier(jnp.mean(values * values, axis=-1, keepdims=True)) + EPSILON)

def matmul(left_op, right_op):
    return jnp.dot(left_op, right_op, precision=lax.Precision.HIGHEST, preferred_element_type=jnp.float32)

def angle_tables(positions, head_dim):
    half_dim = head_dim // 2
    frequency = jnp.power(THETA_BASE, -jnp.arange(half_dim, dtype=jnp.float32) * 2.0 / head_dim)
    angles = positions.astype(jnp.float32)[:, None] * frequency[None, :]
    cosine_tab = jnp.cos(angles)
    sine_tab = jnp.sin(angles)
    return (jnp.concatenate([cosine_tab, cosine_tab], -1), jnp.concatenate([sine_tab, sine_tab], -1))

def rotary(values, cosine_tab, sine_tab):
    half_dim = values.shape[-1] // 2
    turned = jnp.concatenate([-values[..., half_dim:], values[..., :half_dim]], -1)
    return values * cosine_tab + turned * sine_tab

def build_mask(query_pos, key_pos, lengths, pad_len, row_len):
    doc_ends = jnp.cumsum(lengths.astype(jnp.int32))
    query_seg = lax.optimization_barrier(jnp.sum((query_pos[:, None] >= doc_ends[None, :]).astype(jnp.int32), 1))
    key_seg = lax.optimization_barrier(jnp.sum((key_pos[:, None] >= doc_ends[None, :]).astype(jnp.int32), 1))
    valid_key = key_pos < row_len - pad_len
    same_doc = (query_seg[:, None] == key_seg[None, :]) & (key_pos[None, :] <= query_pos[:, None]) & valid_key[None, :]
    return same_doc | (key_pos[None, :] == query_pos[:, None])

def layer_row(params, row_in, lengths, pad_len):
    attn_gain, query_down, query_gain, query_up, key_weight, value_weight, out_weight, ffn_gain, gate_weight, up_weight, down_weight = params
    length = row_in.shape[0]
    positions = jnp.arange(length, dtype=jnp.int32)
    cosine_tab, sine_tab = angle_tables(positions, HEAD_DIM)
    normed = low(row_in * inv_norm(row_in) * attn_gain)
    latent = low_back(matmul(normed, query_down))
    latent_normed = low(latent * inv_norm(latent) * query_gain)
    queries_raw = low_back(matmul(latent_normed, query_up)).reshape(length, HEADS, HEAD_DIM)
    queries = low(rotary(queries_raw, cosine_tab[:, None, :], sine_tab[:, None, :]))
    keys_all = low(rotary(low_back(matmul(normed, key_weight)), cosine_tab, sine_tab))
    values = low(low_back(matmul(normed, value_weight)))
    score_scale = HEAD_DIM ** (-0.5)
    scores = low_back(jnp.einsum('qhd,kd->hqk', queries, keys_all, precision=lax.Precision.HIGHEST) * score_scale)
    allowed = build_mask(positions, positions, lengths, pad_len, length)
    attn_probs = jax.nn.softmax(jnp.where(allowed[None], scores, NEG_FILL), axis=-1)
    mixture = jnp.einsum('hqk,kd->qhd', low(attn_probs), values, precision=lax.Precision.HIGHEST)
    context = low(low_back(mixture)).reshape(length, HEADS * HEAD_DIM)
    resid = row_in + low_back(matmul(context, out_weight))
    ffn_in = low(resid * inv_norm(resid) * ffn_gain)
    gate_proj = low_back(matmul(ffn_in, gate_weight))
    up_proj = low_back(matmul(ffn_in, up_weight))
    hidden = low(jax.nn.silu(gate_proj) * up_proj)
    return resid + low_back(matmul(hidden, down_weight))

def reference(tokens, cotangent, doc_lengths, pad_lengths, attn_gain, query_down, query_gain, query_up, key_weight, value_weight, out_weight, ffn_gain, gate_weight, up_weight, down_weight):
    params = tuple((weight.astype(jnp.float32) for weight in (attn_gain, query_down, query_gain, query_up, key_weight, value_weight, out_weight, ffn_gain, gate_weight, up_weight, down_weight)))
    rows_in = tokens.astype(jnp.float32).reshape(-1, ROW_LEN, D)
    all_lengths = doc_lengths.reshape(-1, NDOC).astype(jnp.int32)
    all_pads = pad_lengths.reshape(-1).astype(jnp.int32)

    def run_rows(params_in, rows):

        def row_step(carried, row_item):
            row_in, lengths, pad_len = row_item
            return (carried, jax.checkpoint(layer_row)(params_in, row_in, lengths, pad_len))
        return lax.scan(row_step, jnp.zeros((), jnp.float32), (rows, all_lengths, all_pads))[1]
    layer_rows, pullback = jax.vjp(run_rows, params, rows_in)
    param_grads, row_grads = pullback(cotangent.astype(jnp.float32).reshape(rows_in.shape))
    return (layer_rows.reshape(tokens.shape).astype(jnp.bfloat16), row_grads.reshape(tokens.shape).astype(jnp.bfloat16), param_grads[0], param_grads[1], param_grads[2], param_grads[3], param_grads[4], param_grads[5], param_grads[6], param_grads[7], param_grads[8], param_grads[9], param_grads[10])
```

```python
import itertools

import jax
import jax.numpy as jnp
from jax import lax
from jax.sharding import PartitionSpec as P

HEAD_DIM = 256
LONGEST = 512

EPSILON = 1e-05
THETA_BASE = 10000.0
NEG_FILL = -1e30

PAIR = 2
CORE = 2
SEQ_DIM, ROW_DIM, PAIR_DIM, CORE_DIM = 0, 1, 2, 3
AXES = ("seq", "dp")
SCORE_SCALE = HEAD_DIM ** (-0.5)

BF = jnp.bfloat16
F32 = jnp.float32


def inv_norm(values):
    return lax.rsqrt(jnp.mean(values * values, axis=-1, keepdims=True) + EPSILON)


def dot_nn(left_op, right_op):
    return jnp.dot(left_op, right_op, preferred_element_type=F32)


def dot_nt(left_op, right_op):
    return lax.dot_general(left_op, right_op, (((1,), (1,)), ((), ())), preferred_element_type=F32)


def dot_tn(left_op, right_op):
    return lax.dot_general(left_op, right_op, (((0,), (0,)), ((), ())), preferred_element_type=F32)


def angle_tables(positions, head_dim):
    half_dim = head_dim // 2
    frequency = jnp.power(THETA_BASE, -jnp.arange(half_dim, dtype=F32) * 2.0 / head_dim)
    angles = positions.astype(F32)[:, None] * frequency[None, :]
    cosine_tab = jnp.cos(angles)
    sine_tab = jnp.sin(angles)
    return (
        jnp.concatenate([cosine_tab, cosine_tab], -1),
        jnp.concatenate([sine_tab, sine_tab], -1),
    )


def rotary(values, cosine_tab, sine_tab):
    half_dim = values.shape[-1] // 2
    turned = jnp.concatenate([-values[..., half_dim:], values[..., :half_dim]], -1)
    return values * cosine_tab + turned * sine_tab


class Places:
    def __init__(self, seq_size, dp_size):
        self.dims = (seq_size, dp_size // (PAIR * CORE), PAIR, CORE)
        self.spots = list(itertools.product(*(range(n) for n in self.dims)))
        self.total = len(self.spots)

    def number(self, spot):
        flat = 0
        for size, at in zip(self.dims, spot):
            flat = flat * size + at
        return flat

    def fetch(self, value, dim, offset, wrap=True):
        if offset == 0:
            return value
        pairs = []
        for spot in self.spots:
            at = spot[dim] + offset
            if not wrap and not 0 <= at < self.dims[dim]:
                continue
            source = spot[:dim] + (at % self.dims[dim],) + spot[dim + 1 :]
            pairs.append((self.number(source), self.number(spot)))
        return lax.ppermute(value, AXES, pairs)

    def head_homes(self, head_blocks):
        pairs = []
        for block in range(self.total):
            head = block // head_blocks
            outer = (head // CORE) * head_blocks + block % head_blocks
            pairs.append((block, outer * CORE + head % CORE))
        return pairs


def absolute(chunks, index, dim):
    count = len(chunks)
    shape = list(chunks[0].shape)
    shape.insert(dim, count)
    turn = (lax.broadcasted_iota(jnp.int32, shape, dim) - index) % count
    value = jnp.expand_dims(chunks[0], dim)
    for k in range(1, count):
        value = jnp.where(turn == k, jnp.expand_dims(chunks[k], dim), value)
    return jnp.broadcast_to(value, shape)


def relative(values, index, dim):
    count = values.shape[dim]
    chunks = [lax.index_in_dim(values, i, dim, keepdims=False) for i in range(count)]
    placed = []
    for k in range(count):
        value = chunks[0]
        for position in range(1, count):
            value = jnp.where((index + k) % count == position, chunks[position], value)
        placed.append(value)
    return placed


def together(*values):
    return lax.optimization_barrier(values)


def ring_gather(places, block):
    blocks = [block]
    for _ in range(1, places.dims[SEQ_DIM]):
        blocks.append(places.fetch(blocks[-1], SEQ_DIM, 1))
    return blocks


def swap_gather(places, value, dim):
    return [places.fetch(value, dim, q) for q in range(places.dims[dim])]


def sum_swaps(places, parts, dim):
    total = parts[0].astype(F32)
    for q in range(1, len(parts)):
        total = total + places.fetch(parts[q].astype(BF), dim, -q).astype(F32)
    return total


def ring_sum(places, parts):
    order = list(range(1, len(parts))) + [0]
    total = parts[order[0]].astype(F32)
    for r in order[1:]:
        total = parts[r].astype(F32) + places.fetch(total.astype(BF), SEQ_DIM, 1).astype(F32)
    return total


def build_mask(query_pos, key_pos, lengths, pad_len, row_len):
    doc_ends = jnp.cumsum(lengths)
    query_seg = jnp.sum((query_pos[:, None] >= doc_ends[None, :]).astype(jnp.int32), 1)
    key_seg = jnp.sum((key_pos[:, None] >= doc_ends[None, :]).astype(jnp.int32), 1)
    valid_key = (key_pos < row_len - pad_len) & (key_pos >= 0)
    same_doc = (
        (query_seg[:, None] == key_seg[None, :])
        & (key_pos[None, :] <= query_pos[:, None])
        & valid_key[None, :]
    )
    return same_doc | (key_pos[None, :] == query_pos[:, None])


def attend(queries, keys, values, allowed):
    scores = jnp.einsum("bqhd,bkd->bhqk", queries, keys, preferred_element_type=F32) * SCORE_SCALE
    scores = jnp.where(allowed[:, None], scores, NEG_FILL)
    peak = jnp.max(scores, axis=-1, keepdims=True)
    expd = jnp.exp(scores - peak)
    total = jnp.sum(expd, axis=-1, keepdims=True)
    probs = expd / total
    mixture = jnp.einsum("bhqk,bkd->bqhd", probs.astype(BF), values, preferred_element_type=F32)
    return mixture.astype(BF), peak + jnp.log(total)


def attend_back(queries, keys, values, allowed, log_total, d_context):
    scores = jnp.einsum("bqhd,bkd->bhqk", queries, keys, preferred_element_type=F32) * SCORE_SCALE
    scores = jnp.where(allowed[:, None], scores, NEG_FILL)
    probs = jnp.exp(scores - log_total)
    d_probs = jnp.einsum("bqhd,bkd->bhqk", d_context, values, preferred_element_type=F32)
    d_values = jnp.einsum("bhqk,bqhd->bkd", probs.astype(BF), d_context, preferred_element_type=F32)
    d_scores = probs * (d_probs - jnp.sum(probs * d_probs, axis=-1, keepdims=True))
    d_scores = d_scores.astype(BF)
    d_queries = (
        jnp.einsum("bhqk,bkd->bqhd", d_scores, keys, preferred_element_type=F32) * SCORE_SCALE
    )
    d_keys = jnp.einsum("bhqk,bqhd->bkd", d_scores, queries, preferred_element_type=F32) * SCORE_SCALE
    return d_queries, d_keys, d_values


def body(
    tokens,
    cotangent,
    doc_lengths,
    pad_lengths,
    attn_gain,
    query_down,
    query_gain,
    query_up,
    key_weight,
    value_weight,
    out_weight,
    ffn_gain,
    gate_weight,
    up_weight,
    down_weight,
):
    places = Places(lax.axis_size("seq"), lax.axis_size("dp"))
    seq_n, row_n, pair_n, core_n = places.dims
    seq_at = lax.axis_index("seq")
    pair_at = (lax.axis_index("dp") // core_n) % pair_n
    row_at = lax.axis_index("dp") // (core_n * pair_n)
    core_at = lax.axis_index("dp") % core_n
    micro, _, local_len, width = tokens.shape
    row_len = local_len * seq_n
    rank = query_down.shape[1]
    head_blocks = HEAD_DIM // query_up.shape[1]
    hidden_block = gate_weight.shape[1]
    shard_rows = query_down.shape[0]

    head_wide = head_blocks > pair_n

    def head_rows(by_row):
        return absolute(by_row, row_at, 1) if head_wide else jnp.stack(by_row, 1)

    def both_cores(value):
        return jnp.stack([value, places.fetch(value, CORE_DIM, 1)], 1)

    gains = jnp.stack(
        [attn_gain, ffn_gain, jnp.pad(query_gain, (0, shard_rows - query_gain.shape[0]))], 1
    )
    gains = jnp.pad(gains, ((0, 0), (0, 128 - gains.shape[1])))
    shared = jnp.concatenate([query_down, key_weight, value_weight, gains], 1)
    homes = places.head_homes(head_blocks)
    up_home = lax.ppermute(query_up.T, AXES, homes)
    out_home = lax.ppermute(out_weight, AXES, homes)
    dys = cotangent[:, 0]
    dy_pair = places.fetch(dys, PAIR_DIM, 1)
    shared_seq = ring_gather(places, shared)
    hs = tokens[:, 0].astype(F32)
    inv_attn = inv_norm(hs)
    lengths_both = both_cores(doc_lengths[:, 0])
    pads_both = both_cores(pad_lengths[:, 0])
    shared_seq, up_home, out_home, inv_attn = together(shared_seq, up_home, out_home, inv_attn)

    shared = absolute(shared_seq, seq_at, 0)
    shared_rows = swap_gather(places, shared, ROW_DIM)
    up_seq = ring_gather(places, up_home)
    shared_rows, up_seq, dy_pair, dys = together(shared_rows, up_seq, dy_pair, dys)

    shared = absolute(shared_rows, row_at, 1)
    shared_pairs = swap_gather(places, shared, PAIR_DIM)
    up_rows = swap_gather(places, jnp.stack(up_seq), ROW_DIM)
    out_seq = ring_gather(places, out_home)
    shared_pairs, up_rows, out_seq = together(shared_pairs, up_rows, out_seq)

    shared = absolute(shared_pairs, pair_at, 2)
    shared = absolute(swap_gather(places, shared, CORE_DIM), core_at, 3)
    up_pairs = swap_gather(places, head_rows(up_rows), PAIR_DIM)
    out_rows = swap_gather(places, jnp.stack(out_seq), ROW_DIM)
    hidden_own = jnp.concatenate([gate_weight.T, up_weight.T, down_weight], 0)
    (shared, hidden_own) = together(shared, hidden_own)
    shared = shared.reshape(width, shared.shape[-1])

    hidden_next = places.fetch(hidden_own, SEQ_DIM, 1)
    kv_end = rank + 2 * HEAD_DIM
    attn_gain_f = shared[:, kv_end].astype(F32)
    ffn_gain_f = shared[:, kv_end + 1].astype(F32)
    query_gain_f = (
        shared[:, kv_end + 2]
        .reshape(places.total, shard_rows)[:, : query_gain.shape[0]]
        .reshape(rank)
        .astype(F32)
    )
    unit_attn = hs * inv_attn
    normed = (unit_attn * attn_gain_f).astype(BF).reshape(micro * local_len, width)
    projected = dot_nn(normed, shared[:, :kv_end])
    latent = projected[:, :rank]
    inv_latent = inv_norm(latent)
    unit_latent = latent * inv_latent
    latent_normed = (unit_latent * query_gain_f).astype(BF)
    query_pos = seq_at * local_len + jnp.arange(local_len, dtype=jnp.int32)
    cosine, sine = angle_tables(query_pos, HEAD_DIM)
    keys_own = rotary(
        projected[:, rank : rank + HEAD_DIM].reshape(micro, local_len, HEAD_DIM), cosine, sine
    ).astype(BF)
    values_own = projected[:, rank + HEAD_DIM :].astype(BF).reshape(micro, local_len, HEAD_DIM)
    kv_own = jnp.concatenate([keys_own, values_own], -1)

    spans = min(seq_n, 1 + -(-(LONGEST - 1) // local_len))
    kv_row = jnp.stack(
        [places.fetch(kv_own, SEQ_DIM, -k, wrap=False) for k in reversed(range(spans))], 1
    ).reshape(micro, spans * local_len, 2 * HEAD_DIM)
    kv_both = both_cores(kv_row)
    latent_both = both_cores(latent_normed.reshape(micro, local_len, rank))
    key_pos = (seq_at - (spans - 1)) * local_len + jnp.arange(spans * local_len, dtype=jnp.int32)
    masks = jax.vmap(
        jax.vmap(lambda lengths, pad: build_mask(query_pos, key_pos, lengths, pad, row_len))
    )(lengths_both, pads_both)
    up_pairs, kv_both, latent_both, out_rows, hidden_next = together(
        up_pairs, kv_both, latent_both, out_rows, hidden_next
    )

    out_pairs = swap_gather(places, head_rows(out_rows), PAIR_DIM)
    hidden_blocks = [hidden_own] + ring_gather(places, hidden_next)[: seq_n - 1]
    hidden_rows = [swap_gather(places, a, ROW_DIM) for a in hidden_blocks]
    query_up_t = absolute(up_pairs, pair_at, 2).reshape(-1, rank)
    heads = query_up_t.shape[0] // HEAD_DIM
    attended = []
    for m in range(micro):
        keys_m, values_m = kv_both[m, :, :, :HEAD_DIM], kv_both[m, :, :, HEAD_DIM:]
        latent_m = latent_both[m].reshape(core_n * local_len, rank)
        raw = dot_nt(latent_m, query_up_t).reshape(core_n, local_len, heads, HEAD_DIM)
        queries = rotary(raw, cosine[:, None, :], sine[:, None, :]).astype(BF)
        context, log_total = attend(queries, keys_m, values_m, masks[m])
        context = context.reshape(core_n * local_len, heads * HEAD_DIM)
        attended.append((queries, keys_m, values_m, log_total, context, latent_m))
    out_pairs, attended, hidden_first = together(out_pairs, attended, hidden_rows[0])
    hidden_rows[0] = hidden_first

    out_full = absolute(out_pairs, pair_at, 2).reshape(-1, width)

    def group_cores(value, other):
        two = jnp.stack([value, other])
        return jnp.concatenate([two, places.fetch(two, CORE_DIM, 1)])

    ffn_state = []
    ffn_rows = []
    for m in range(micro):
        part = dot_nn(attended[m][4], out_full).reshape(core_n, local_len, width)
        resid = hs[m] + part[0] + places.fetch(part[1].astype(BF), CORE_DIM, 1).astype(F32)
        inv_ffn = inv_norm(resid)
        unit_ffn = resid * inv_ffn
        ffn_in = (unit_ffn * ffn_gain_f).astype(BF)
        ffn_state.append((resid, inv_ffn, unit_ffn))
        ffn_rows.append(group_cores(ffn_in, places.fetch(ffn_in, PAIR_DIM, 1)))
    ffn_rows = jnp.stack(ffn_rows, 1).reshape(-1, width)
    dy_rows = group_cores(dys, dy_pair).reshape(-1, width)
    ffn_rows, dy_rows, hidden_rows = together(ffn_rows, dy_rows, hidden_rows)
    gate_t, up_t, down_t = (
        jnp.concatenate(
            [a[k * hidden_block : (k + 1) * hidden_block] for by_row in hidden_rows for a in by_row],
            0,
        )
        for k in range(3)
    )

    def hidden_parts(grad):
        grad = grad.reshape(seq_n, row_n, hidden_block, width)
        return [grad[:, q] for q in range(row_n)]

    def group_scatter_core(part):
        part = part.reshape(core_n, pair_n, micro, local_len, width)
        return part[0] + places.fetch(part[1].astype(BF), CORE_DIM, 1).astype(F32)

    gate = dot_nt(ffn_rows, gate_t)
    up = dot_nt(ffn_rows, up_t)
    sig = jax.nn.sigmoid(gate)
    hidden = (gate * sig * up).astype(BF)
    d_hidden = dot_nt(dy_rows, down_t)
    d_gate = (d_hidden * up * (sig * (1.0 + gate * (1.0 - sig)))).astype(BF)
    d_up = (d_hidden * (gate * sig)).astype(BF)
    down_grad = dot_tn(hidden, dy_rows).astype(BF)
    d_gate, d_up, down_grad = together(d_gate, d_up, down_grad)

    down_sums = hidden_parts(down_grad)
    down_away = [places.fetch(down_sums[q], ROW_DIM, -q) for q in range(1, row_n)]
    d_ffn_half = group_scatter_core(dot_nn(d_gate, gate_t) + dot_nn(d_up, up_t))
    d_ffn_half, hidden = together(d_ffn_half, hidden)
    d_ffn_away = places.fetch(d_ffn_half[1].astype(BF), PAIR_DIM, 1)
    gate_grad = dot_tn(d_gate, ffn_rows).astype(BF)
    up_grad = dot_tn(d_up, ffn_rows).astype(BF)
    out_half = group_scatter_core(dot_nn(hidden, down_t))
    d_ffn_away, gate_grad, up_grad, out_half = together(d_ffn_away, gate_grad, up_grad, out_half)
    gate_sums, up_sums = hidden_parts(gate_grad), hidden_parts(up_grad)
    gate_away = [places.fetch(gate_sums[q], ROW_DIM, -q) for q in range(1, row_n)]
    up_away = [places.fetch(up_sums[q], ROW_DIM, -q) for q in range(1, row_n)]

    resid, inv_ffn, unit_ffn = (jnp.stack(a) for a in zip(*ffn_state))
    d_ffn_in = d_ffn_half[0] + d_ffn_away.astype(F32)
    ffn_gain_grad = jnp.sum(d_ffn_in * unit_ffn, axis=(0, 1))
    scaled = d_ffn_in * ffn_gain_f
    d_resid = dys.astype(F32) + inv_ffn * (
        scaled - unit_ffn * jnp.mean(scaled * unit_ffn, axis=-1, keepdims=True)
    )
    d_low_both = both_cores(d_resid.astype(BF))
    context_all = jnp.concatenate([a[4] for a in attended], 0)
    out_grad = dot_tn(context_all, d_low_both.reshape(-1, width)).astype(BF)
    out_grad, d_low_both, down_away = together(out_grad, d_low_both, down_away)

    def seq_parts(own, away):
        total = own.astype(F32)
        for a in away:
            total = total + a.astype(F32)
        return [total[r] for r in range(seq_n)]

    def head_pairs(grad):
        return relative(grad.reshape(seq_n, row_n, pair_n, -1, grad.shape[-1]), pair_at, 2)

    def head_row_parts(total):
        if head_wide:
            return relative(total, row_at, 1)
        return [total[:, q] for q in range(row_n)]

    def head_finish(total):
        back = [(dst, src) for src, dst in homes]
        total = ring_sum(places, [total[r] for r in range(seq_n)])
        return lax.ppermute(total.astype(BF), AXES, back).astype(F32)

    out_parts = head_pairs(out_grad)
    out_away = places.fetch(out_parts[1], PAIR_DIM, -1)
    down_grad = ring_sum(places, seq_parts(down_sums[0], down_away))
    d_latents = []
    d_kvs = []
    query_pairs = []
    for m in range(micro):
        queries, keys_m, values_m, log_total, context, latent_m = attended[m]
        d_low = d_low_both[m].reshape(-1, width)
        d_context = (
            dot_nt(d_low, out_full).astype(BF).reshape(core_n, local_len, heads, HEAD_DIM)
        )
        d_queries, d_keys, d_values = attend_back(
            queries, keys_m, values_m, masks[m], log_total, d_context
        )
        d_raw = rotary(d_queries, cosine[:, None, :], -sine[:, None, :]).astype(BF)
        d_raw = d_raw.reshape(core_n * local_len, heads * HEAD_DIM)
        part = dot_nn(d_raw, query_up_t).reshape(core_n, local_len, rank)
        d_latents.append(part[0] + places.fetch(part[1].astype(BF), CORE_DIM, 1).astype(F32))
        d_kv = jnp.concatenate([d_keys, d_values], -1)
        d_kv = d_kv[0] + places.fetch(d_kv[1].astype(BF), CORE_DIM, 1).astype(F32)
        d_kvs.append(d_kv.reshape(spans, local_len, 2 * HEAD_DIM))
        query_pairs.append((d_raw, latent_m))
    d_raw_all, latent_all = (jnp.concatenate(a, 0) for a in zip(*query_pairs))
    d_latents, d_kvs, d_raw_all, out_away, gate_away = together(
        d_latents, d_kvs, d_raw_all, out_away, gate_away
    )

    gate_grad = ring_sum(places, seq_parts(gate_sums[0], gate_away))
    d_kv_all = jnp.stack(d_kvs)
    d_own = d_kv_all[:, spans - 1]
    for k in range(1, spans):
        d_own = d_own + places.fetch(
            d_kv_all[:, spans - 1 - k].astype(BF), SEQ_DIM, k, wrap=False
        ).astype(F32)
    d_latent_normed = jnp.concatenate(d_latents, 0)
    query_gain_grad = jnp.sum(d_latent_normed * unit_latent, axis=0)
    scaled = d_latent_normed * query_gain_f
    d_latent = (
        inv_latent * (scaled - unit_latent * jnp.mean(scaled * unit_latent, axis=-1, keepdims=True))
    ).astype(BF)
    d_key_raw = rotary(d_own[..., :HEAD_DIM], cosine, -sine).astype(BF)
    d_kv_low = jnp.concatenate([d_key_raw, d_own[..., HEAD_DIM:].astype(BF)], -1)
    d_kv_low = d_kv_low.reshape(micro * local_len, 2 * HEAD_DIM)
    d_both = jnp.concatenate([d_latent, d_kv_low], 1)
    shared_grad = dot_tn(normed, d_both)
    d_normed = dot_nt(d_both, shared[:, :kv_end]).reshape(micro, local_len, width)
    attn_gain_grad = jnp.sum(d_normed * unit_attn, axis=(0, 1))
    gain_grads = jnp.stack(
        [
            attn_gain_grad,
            ffn_gain_grad,
            jnp.pad(
                query_gain_grad.reshape(places.total, -1),
                ((0, 0), (0, shard_rows - query_gain.shape[0])),
            ).reshape(width),
        ],
        1,
    )
    gain_grads = jnp.pad(gain_grads, ((0, 0), (0, 128 - gain_grads.shape[1])))
    parts = jnp.concatenate([shared_grad.astype(BF), gain_grads.astype(BF)], 1)
    parts = parts.reshape(*places.dims, shard_rows, -1)
    core_parts = relative(parts, core_at, 3)
    query_up_grad = dot_tn(d_raw_all, latent_all).astype(BF)

    parts = sum_swaps(places, core_parts, CORE_DIM)
    parts = sum_swaps(places, relative(parts, pair_at, 2), PAIR_DIM)
    parts = sum_swaps(places, relative(parts, row_at, 1), ROW_DIM)
    shared_grad = ring_sum(places, relative(parts, seq_at, 0))

    total = out_parts[0].astype(F32) + out_away.astype(F32)
    out_grad = head_finish(sum_swaps(places, head_row_parts(total), ROW_DIM))
    total = sum_swaps(places, head_pairs(query_up_grad), PAIR_DIM)
    query_up_grad = head_finish(sum_swaps(places, head_row_parts(total), ROW_DIM)).T
    up_grad = ring_sum(places, seq_parts(up_sums[0], up_away))

    scaled = d_normed * attn_gain_f
    d_row = inv_attn * (
        scaled - unit_attn * jnp.mean(scaled * unit_attn, axis=-1, keepdims=True)
    )
    tokens_grad = (d_resid + d_row).astype(BF)
    layer_part = out_half[0] + places.fetch(out_half[1].astype(BF), PAIR_DIM, 1).astype(F32)
    layer_rows = (resid + layer_part).astype(BF)

    return (
        layer_rows[:, None],
        tokens_grad[:, None],
        shared_grad[:, kv_end],
        shared_grad[:, :rank],
        shared_grad[: query_gain.shape[0], kv_end + 2],
        query_up_grad,
        shared_grad[:, rank : rank + HEAD_DIM],
        shared_grad[:, rank + HEAD_DIM : kv_end],
        out_grad,
        shared_grad[:, kv_end + 1],
        gate_grad.T,
        up_grad.T,
        down_grad,
    )


def solution(mesh):
    whole = P(AXES)
    rows = P(AXES, None)
    columns = P(None, AXES)
    packed = P(None, "dp", "seq", None)
    return jax.shard_map(
        body,
        mesh=mesh,
        in_specs=(
            packed,
            packed,
            P(None, "dp", None),
            P(None, "dp"),
            whole,
            rows,
            whole,
            columns,
            rows,
            rows,
            rows,
            whole,
            columns,
            columns,
            rows,
        ),
        out_specs=(
            packed,
            packed,
            whole,
            rows,
            whole,
            columns,
            rows,
            rows,
            rows,
            whole,
            columns,
            columns,
            rows,
        ),
        check_vma=False,
    )
```

```python
import itertools

import jax
import jax.numpy as jnp
from jax import lax
from jax.sharding import PartitionSpec as P

HEAD_DIM = 256
LONGEST = 512

EPSILON = 1e-05
THETA_BASE = 10000.0
NEG_FILL = -1e30

PAIR = 2
CORE = 2
SEQ_DIM, ROW_DIM, PAIR_DIM, CORE_DIM = 0, 1, 2, 3
AXES = ("seq", "dp")
SCORE_SCALE = HEAD_DIM ** (-0.5)

BF = jnp.bfloat16
F32 = jnp.float32


def inv_norm(values):
    return lax.rsqrt(jnp.mean(values * values, axis=-1, keepdims=True) + EPSILON)


def dot_nn(left_op, right_op):
    return jnp.dot(left_op, right_op, preferred_element_type=F32)


def dot_nt(left_op, right_op):
    return lax.dot_general(left_op, right_op, (((1,), (1,)), ((), ())), preferred_element_type=F32)


def dot_tn(left_op, right_op):
    return lax.dot_general(left_op, right_op, (((0,), (0,)), ((), ())), preferred_element_type=F32)


def angle_tables(positions, head_dim):
    half_dim = head_dim // 2
    frequency = jnp.power(THETA_BASE, -jnp.arange(half_dim, dtype=F32) * 2.0 / head_dim)
    angles = positions.astype(F32)[:, None] * frequency[None, :]
    cosine_tab = jnp.cos(angles)
    sine_tab = jnp.sin(angles)
    return (
        jnp.concatenate([cosine_tab, cosine_tab], -1),
        jnp.concatenate([sine_tab, sine_tab], -1),
    )


def rotary(values, cosine_tab, sine_tab):
    half_dim = values.shape[-1] // 2
    turned = jnp.concatenate([-values[..., half_dim:], values[..., :half_dim]], -1)
    return values * cosine_tab + turned * sine_tab


class Places:
    def __init__(self, seq_size, dp_size):
        self.dims = (seq_size, dp_size // (PAIR * CORE), PAIR, CORE)
        self.spots = list(itertools.product(*(range(n) for n in self.dims)))
        self.total = len(self.spots)

    def number(self, spot):
        flat = 0
        for size, at in zip(self.dims, spot):
            flat = flat * size + at
        return flat

    def fetch(self, value, dim, offset, wrap=True):
        if offset == 0:
            return value
        pairs = []
        for spot in self.spots:
            at = spot[dim] + offset
            if not wrap and not 0 <= at < self.dims[dim]:
                continue
            source = spot[:dim] + (at % self.dims[dim],) + spot[dim + 1 :]
            pairs.append((self.number(source), self.number(spot)))
        return lax.ppermute(value, AXES, pairs)

    def head_homes(self, head_blocks):
        pairs = []
        for block in range(self.total):
            head = block // head_blocks
            outer = (head // CORE) * head_blocks + block % head_blocks
            pairs.append((block, outer * CORE + head % CORE))
        return pairs


def absolute(chunks, index, dim):
    count = len(chunks)
    shape = list(chunks[0].shape)
    shape.insert(dim, count)
    turn = (lax.broadcasted_iota(jnp.int32, shape, dim) - index) % count
    value = jnp.expand_dims(chunks[0], dim)
    for k in range(1, count):
        value = jnp.where(turn == k, jnp.expand_dims(chunks[k], dim), value)
    return jnp.broadcast_to(value, shape)


def relative(values, index, dim):
    count = values.shape[dim]
    chunks = [lax.index_in_dim(values, i, dim, keepdims=False) for i in range(count)]
    placed = []
    for k in range(count):
        value = chunks[0]
        for position in range(1, count):
            value = jnp.where((index + k) % count == position, chunks[position], value)
        placed.append(value)
    return placed


def together(*values):
    return lax.optimization_barrier(values)


def seq_gather(places, block):
    return [places.fetch(block, SEQ_DIM, r) for r in range(places.dims[SEQ_DIM])]


def swap_gather(places, value, dim):
    return [places.fetch(value, dim, q) for q in range(places.dims[dim])]


def sum_swaps(places, parts, dim):
    total = parts[0].astype(F32)
    for q in range(1, len(parts)):
        total = total + places.fetch(parts[q].astype(BF), dim, -q).astype(F32)
    return total


def seq_sum(places, parts):
    total = parts[0].astype(F32)
    for r in range(1, len(parts)):
        total = total + places.fetch(parts[r].astype(BF), SEQ_DIM, -r).astype(F32)
    return total


def row_away(places, parts):
    return [places.fetch(parts[q], ROW_DIM, -1 - q) for q in range(len(parts))]


def row_total(own, came):
    total = own.astype(F32)
    for value in came:
        total = total + value.astype(F32)
    return total


def seq_away(places, total):
    return [places.fetch(total[r].astype(BF), SEQ_DIM, -r) for r in range(1, total.shape[0])]


def build_mask(query_pos, key_pos, lengths, pad_len, row_len):
    doc_ends = jnp.cumsum(lengths)
    query_seg = jnp.sum((query_pos[:, None] >= doc_ends[None, :]).astype(jnp.int32), 1)
    key_seg = jnp.sum((key_pos[:, None] >= doc_ends[None, :]).astype(jnp.int32), 1)
    valid_key = (key_pos < row_len - pad_len) & (key_pos >= 0)
    same_doc = (
        (query_seg[:, None] == key_seg[None, :])
        & (key_pos[None, :] <= query_pos[:, None])
        & valid_key[None, :]
    )
    return same_doc | (key_pos[None, :] == query_pos[:, None])


def attend(queries, keys, values, allowed):
    scores = jnp.einsum("bqhd,bkd->bhqk", queries, keys, preferred_element_type=F32) * SCORE_SCALE
    scores = jnp.where(allowed[:, None], scores, NEG_FILL)
    peak = jnp.max(scores, axis=-1, keepdims=True)
    expd = jnp.exp(scores - peak)
    total = jnp.sum(expd, axis=-1, keepdims=True)
    probs = expd / total
    mixture = jnp.einsum("bhqk,bkd->bqhd", probs.astype(BF), values, preferred_element_type=F32)
    return mixture.astype(BF), peak + jnp.log(total)


def attend_back(queries, keys, values, allowed, log_total, d_context):
    scores = jnp.einsum("bqhd,bkd->bhqk", queries, keys, preferred_element_type=F32) * SCORE_SCALE
    scores = jnp.where(allowed[:, None], scores, NEG_FILL)
    probs = jnp.exp(scores - log_total)
    d_probs = jnp.einsum("bqhd,bkd->bhqk", d_context, values, preferred_element_type=F32)
    d_values = jnp.einsum("bhqk,bqhd->bkd", probs.astype(BF), d_context, preferred_element_type=F32)
    d_scores = probs * (d_probs - jnp.sum(probs * d_probs, axis=-1, keepdims=True))
    d_scores = d_scores.astype(BF)
    d_queries = (
        jnp.einsum("bhqk,bkd->bqhd", d_scores, keys, preferred_element_type=F32) * SCORE_SCALE
    )
    d_keys = jnp.einsum("bhqk,bqhd->bkd", d_scores, queries, preferred_element_type=F32) * SCORE_SCALE
    return d_queries, d_keys, d_values


def body(
    tokens,
    cotangent,
    doc_lengths,
    pad_lengths,
    attn_gain,
    query_down,
    query_gain,
    query_up,
    key_weight,
    value_weight,
    out_weight,
    ffn_gain,
    gate_weight,
    up_weight,
    down_weight,
):
    places = Places(lax.axis_size("seq"), lax.axis_size("dp"))
    seq_n, row_n, pair_n, core_n = places.dims
    seq_at = lax.axis_index("seq")
    pair_at = (lax.axis_index("dp") // core_n) % pair_n
    row_at = lax.axis_index("dp") // (core_n * pair_n)
    core_at = lax.axis_index("dp") % core_n
    micro, _, local_len, width = tokens.shape
    row_len = local_len * seq_n
    rank = query_down.shape[1]
    head_blocks = HEAD_DIM // query_up.shape[1]
    hidden_block = gate_weight.shape[1]
    shard_rows = query_down.shape[0]

    head_wide = head_blocks > pair_n

    def head_rows(by_row):
        return absolute(by_row, row_at, 1) if head_wide else jnp.stack(by_row, 1)

    def both_cores(value):
        return jnp.stack([value, places.fetch(value, CORE_DIM, 1)], 1)

    gains = jnp.stack(
        [attn_gain, ffn_gain, jnp.pad(query_gain, (0, shard_rows - query_gain.shape[0]))], 1
    )
    gains = jnp.pad(gains, ((0, 0), (0, 128 - gains.shape[1])))
    shared = jnp.concatenate([query_down, key_weight, value_weight, gains], 1)
    homes = places.head_homes(head_blocks)
    up_home = lax.ppermute(query_up.T, AXES, homes)
    out_home = lax.ppermute(out_weight, AXES, homes)
    dys = cotangent[:, 0]
    shared_seq = seq_gather(places, shared)
    hs = tokens[:, 0].astype(F32)
    inv_attn = inv_norm(hs)
    lengths_both = both_cores(doc_lengths[:, 0])
    pads_both = both_cores(pad_lengths[:, 0])
    hidden_own = jnp.concatenate([gate_weight.T, up_weight.T, down_weight], 0)
    shared_seq, up_home, out_home, inv_attn, hidden_own = together(
        shared_seq, up_home, out_home, inv_attn, hidden_own
    )

    shared = absolute(shared_seq, seq_at, 0)
    shared_rows = swap_gather(places, shared, ROW_DIM)
    up_seq = seq_gather(places, up_home)
    out_seq = seq_gather(places, out_home)
    shared_rows, up_seq, hidden_own = together(shared_rows, up_seq, hidden_own)

    shared = absolute(shared_rows, row_at, 1)
    shared_pairs = swap_gather(places, shared, PAIR_DIM)
    up_rows = swap_gather(places, jnp.stack(up_seq), ROW_DIM)
    shared_pairs, up_rows = together(shared_pairs, up_rows)

    shared = absolute(shared_pairs, pair_at, 2)
    shared = absolute(swap_gather(places, shared, CORE_DIM), core_at, 3)
    up_pairs = swap_gather(places, head_rows(up_rows), PAIR_DIM)
    shared, out_seq = together(shared, out_seq)
    shared = shared.reshape(width, shared.shape[-1])

    out_rows = swap_gather(places, jnp.stack(out_seq), ROW_DIM)
    kv_end = rank + 2 * HEAD_DIM
    attn_gain_f = shared[:, kv_end].astype(F32)
    ffn_gain_f = shared[:, kv_end + 1].astype(F32)
    query_gain_f = (
        shared[:, kv_end + 2]
        .reshape(places.total, shard_rows)[:, : query_gain.shape[0]]
        .reshape(rank)
        .astype(F32)
    )
    unit_attn = hs * inv_attn
    normed = (unit_attn * attn_gain_f).astype(BF).reshape(micro * local_len, width)
    projected = dot_nn(normed, shared[:, :kv_end])

    def across_rows(block):
        return [places.fetch(block, ROW_DIM, q) for q in range(1, row_n)]

    latent = projected[:, :rank]
    inv_latent = inv_norm(latent)
    unit_latent = latent * inv_latent
    latent_normed = (unit_latent * query_gain_f).astype(BF)
    query_pos = seq_at * local_len + jnp.arange(local_len, dtype=jnp.int32)
    cosine, sine = angle_tables(query_pos, HEAD_DIM)
    keys_own = rotary(
        projected[:, rank : rank + HEAD_DIM].reshape(micro, local_len, HEAD_DIM), cosine, sine
    ).astype(BF)
    values_own = projected[:, rank + HEAD_DIM :].astype(BF).reshape(micro, local_len, HEAD_DIM)
    kv_own = jnp.concatenate([keys_own, values_own], -1)

    spans = min(seq_n, 1 + -(-(LONGEST - 1) // local_len))
    kv_row = [places.fetch(kv_own, SEQ_DIM, -k, wrap=False) for k in reversed(range(spans))]
    kv_row, out_heads, hidden_own = together(kv_row, head_rows(out_rows), hidden_own)
    out_pairs = swap_gather(places, out_heads, PAIR_DIM)
    hidden_ring = [hidden_own, places.fetch(hidden_own, SEQ_DIM, 1)]
    hidden_far = [across_rows(hidden_own)]
    kv_row = jnp.stack(kv_row, 1).reshape(micro, spans * local_len, 2 * HEAD_DIM)
    kv_both = both_cores(kv_row)
    latent_both = both_cores(latent_normed.reshape(micro, local_len, rank))
    key_pos = (seq_at - (spans - 1)) * local_len + jnp.arange(spans * local_len, dtype=jnp.int32)
    masks = jax.vmap(
        jax.vmap(lambda lengths, pad: build_mask(query_pos, key_pos, lengths, pad, row_len))
    )(lengths_both, pads_both)
    up_pairs, kv_both, latent_both, dys, hidden_ring, hidden_far = together(
        up_pairs, kv_both, latent_both, dys, hidden_ring, hidden_far
    )

    dy_pair = places.fetch(dys, PAIR_DIM, 1)
    query_up_t = absolute(up_pairs, pair_at, 2).reshape(-1, rank)
    heads = query_up_t.shape[0] // HEAD_DIM

    def group_cores(value, other):
        two = jnp.stack([value, other])
        return jnp.concatenate([two, places.fetch(two, CORE_DIM, 1)])


    def hidden_on(ring, far):
        return ring + [places.fetch(ring[-1], SEQ_DIM, 1)], far + [across_rows(ring[-1])]

    hidden_ring, hidden_far = hidden_on(hidden_ring, hidden_far)
    attended = []
    ffn_state = []
    ffn_rows = []
    for m in range(micro):
        keys_m, values_m = kv_both[m, :, :, :HEAD_DIM], kv_both[m, :, :, HEAD_DIM:]
        latent_m = latent_both[m].reshape(core_n * local_len, rank)
        raw = dot_nt(latent_m, query_up_t).reshape(core_n, local_len, heads, HEAD_DIM)
        queries = rotary(raw, cosine[:, None, :], sine[:, None, :]).astype(BF)
        context, log_total = attend(queries, keys_m, values_m, masks[m])
        context = context.reshape(core_n * local_len, heads * HEAD_DIM)
        if m == 0:
            context, out_pairs, hidden_ring, hidden_far = together(
                context, out_pairs, hidden_ring, hidden_far
            )
            out_full = absolute(out_pairs, pair_at, 2).reshape(-1, width)
        else:
            context, dy_pair, hidden_ring, hidden_far = together(
                context, dy_pair, hidden_ring, hidden_far
            )
        while len(hidden_ring) < seq_n and (m == 0 or m == micro - 1):
            hidden_ring, hidden_far = hidden_on(hidden_ring, hidden_far)
            if m == 0:
                break
        attended.append((queries, keys_m, values_m, log_total, context, latent_m))
        part = [
            dot_nn(context[k * local_len : (k + 1) * local_len], out_full) for k in range(core_n)
        ]
        resid = hs[m] + part[0] + places.fetch(part[1].astype(BF), CORE_DIM, 1).astype(F32)
        inv_ffn = inv_norm(resid)
        unit_ffn = resid * inv_ffn
        ffn_in = (unit_ffn * ffn_gain_f).astype(BF)
        ffn_in, kv_both, latent_both = together(ffn_in, kv_both, latent_both)
        ffn_state.append((resid, inv_ffn, unit_ffn))
        ffn_rows.append((ffn_in, places.fetch(ffn_in, PAIR_DIM, 1)))

    hidden_far.append(across_rows(hidden_ring[-1]))
    ffn_rows, hidden_far = together(ffn_rows, hidden_far)
    ffn_rows = jnp.stack([group_cores(*a) for a in ffn_rows], 1).reshape(-1, width)
    dy_rows = group_cores(dys, dy_pair).reshape(-1, width)
    ffn_rows, dy_rows = together(ffn_rows, dy_rows)
    gate_t, up_t, down_t = (
        jnp.concatenate(
            [
                a[k * hidden_block : (k + 1) * hidden_block]
                for own, far in zip(hidden_ring, hidden_far)
                for a in [own] + far
            ],
            0,
        )
        for k in range(3)
    )

    def far_parts(grad):
        grad = grad.reshape(seq_n, row_n, hidden_block, width)
        return [grad[:, q] for q in range(1, row_n)]

    def own_parts(grad):
        return grad.reshape(seq_n, row_n, hidden_block, width)[:, 0]

    half_rows = pair_n * micro * local_len

    def group_scatter_core(part):
        away = part(slice(half_rows, None)).astype(BF)
        total = part(slice(0, half_rows)) + places.fetch(away, CORE_DIM, 1).astype(F32)
        return total.reshape(pair_n, micro, local_len, width)

    gate = dot_nt(ffn_rows, gate_t)
    up = dot_nt(ffn_rows, up_t)
    sig = jax.nn.sigmoid(gate)
    hidden = (gate * sig * up).astype(BF)
    d_hidden = dot_nt(dy_rows, down_t)
    d_gate = (d_hidden * up * (sig * (1.0 + gate * (1.0 - sig)))).astype(BF)
    d_up = (d_hidden * (gate * sig)).astype(BF)
    down_grad = dot_tn(hidden, dy_rows).astype(BF)
    d_gate, d_up, hidden, down_grad = together(d_gate, d_up, hidden, down_grad)

    down_came = row_away(places, far_parts(down_grad))
    d_ffn_half = group_scatter_core(
        lambda rows: dot_nn(d_gate[rows], gate_t) + dot_nn(d_up[rows], up_t)
    )
    d_ffn_out = d_ffn_half[1].astype(BF)
    d_ffn_half, d_ffn_out, hidden, d_gate, d_up = together(
        d_ffn_half, d_ffn_out, hidden, d_gate, d_up
    )
    d_ffn_away = places.fetch(d_ffn_out, PAIR_DIM, 1)
    gate_grad = dot_tn(d_gate, ffn_rows).astype(BF)
    up_grad = dot_tn(d_up, ffn_rows).astype(BF)
    d_ffn_away, gate_grad, up_grad, hidden, down_came = together(
        d_ffn_away, gate_grad, up_grad, hidden, down_came
    )
    gate_came = row_away(places, far_parts(gate_grad))
    down_total = row_total(own_parts(down_grad), down_came)
    down_came = seq_away(places, down_total)
    out_half = group_scatter_core(lambda rows: dot_nn(hidden[rows], down_t))

    resid, inv_ffn, unit_ffn = (jnp.stack(a) for a in zip(*ffn_state))
    d_ffn_in = d_ffn_half[0] + d_ffn_away.astype(F32)
    ffn_gain_grad = jnp.sum(d_ffn_in * unit_ffn, axis=(0, 1))
    scaled = d_ffn_in * ffn_gain_f
    d_resid = dys.astype(F32) + inv_ffn * (
        scaled - unit_ffn * jnp.mean(scaled * unit_ffn, axis=-1, keepdims=True)
    )
    d_low_both = both_cores(d_resid.astype(BF))
    context_all = jnp.concatenate([a[4] for a in attended], 0)
    out_grad = dot_tn(context_all, d_low_both.reshape(-1, width)).astype(BF)
    out_grad, d_low_both, up_grad, out_half, gate_came = together(
        out_grad, d_low_both, up_grad, out_half, gate_came
    )
    up_came = row_away(places, far_parts(up_grad))
    gate_total = row_total(own_parts(gate_grad), gate_came)
    out_pair_away = places.fetch(out_half[1].astype(BF), PAIR_DIM, 1)

    def head_pairs(grad):
        return relative(grad.reshape(seq_n, row_n, pair_n, -1, grad.shape[-1]), pair_at, 2)

    def head_row_parts(total):
        if head_wide:
            return relative(total, row_at, 1)
        return [total[:, q] for q in range(row_n)]

    def head_finish(total):
        back = [(dst, src) for src, dst in homes]
        total = seq_sum(places, [total[r] for r in range(seq_n)])
        return lax.ppermute(total.astype(BF), AXES, back).astype(F32)

    out_parts = head_pairs(out_grad)
    out_away = places.fetch(out_parts[1], PAIR_DIM, -1)
    d_latents = []
    d_kvs = []
    query_pairs = []
    for m in range(micro):
        queries, keys_m, values_m, log_total, context, latent_m = attended[m]
        d_low = d_low_both[m].reshape(-1, width)
        d_context = (
            dot_nt(d_low, out_full).astype(BF).reshape(core_n, local_len, heads, HEAD_DIM)
        )
        d_queries, d_keys, d_values = attend_back(
            queries, keys_m, values_m, masks[m], log_total, d_context
        )
        d_raw = rotary(d_queries, cosine[:, None, :], -sine[:, None, :]).astype(BF)
        d_raw = d_raw.reshape(core_n * local_len, heads * HEAD_DIM)
        part = dot_nn(d_raw, query_up_t).reshape(core_n, local_len, rank)
        d_latents.append(part[0] + places.fetch(part[1].astype(BF), CORE_DIM, 1).astype(F32))
        d_kv = jnp.concatenate([d_keys, d_values], -1)
        d_kv = d_kv[0] + places.fetch(d_kv[1].astype(BF), CORE_DIM, 1).astype(F32)
        d_kvs.append(d_kv.reshape(spans, local_len, 2 * HEAD_DIM))
        if m == 0:
            d_raw, d_latents, d_kvs, up_came, down_came, out_pair_away, d_low_both = together(
                d_raw, d_latents, d_kvs, up_came, down_came, out_pair_away, d_low_both
            )
            gate_came = seq_away(places, gate_total)
            up_total = row_total(own_parts(up_grad), up_came)
        query_pairs.append((d_raw, latent_m))
    d_raw_all, latent_all = (jnp.concatenate(a, 0) for a in zip(*query_pairs))
    d_latents, d_kvs, d_raw_all, out_away, gate_came, up_total = together(
        d_latents, d_kvs, d_raw_all, out_away, gate_came, up_total
    )

    up_came = seq_away(places, up_total)
    total = out_parts[0].astype(F32) + out_away.astype(F32)
    out_rows_grad = head_row_parts(total)
    out_row_away = [
        places.fetch(out_rows_grad[q].astype(BF), ROW_DIM, -q) for q in range(1, row_n)
    ]
    d_kv_all = jnp.stack(d_kvs)
    d_own = d_kv_all[:, spans - 1]
    for k in range(1, spans):
        d_own = d_own + places.fetch(
            d_kv_all[:, spans - 1 - k].astype(BF), SEQ_DIM, k, wrap=False
        ).astype(F32)
    d_latent_normed = jnp.concatenate(d_latents, 0)
    query_gain_grad = jnp.sum(d_latent_normed * unit_latent, axis=0)
    scaled = d_latent_normed * query_gain_f
    d_latent = (
        inv_latent * (scaled - unit_latent * jnp.mean(scaled * unit_latent, axis=-1, keepdims=True))
    ).astype(BF)
    d_key_raw = rotary(d_own[..., :HEAD_DIM], cosine, -sine).astype(BF)
    d_kv_low = jnp.concatenate([d_key_raw, d_own[..., HEAD_DIM:].astype(BF)], -1)
    d_kv_low = d_kv_low.reshape(micro * local_len, 2 * HEAD_DIM)
    d_both = jnp.concatenate([d_latent, d_kv_low], 1)
    shared_grad = dot_tn(normed, d_both)
    d_normed = dot_nt(d_both, shared[:, :kv_end]).reshape(micro, local_len, width)
    attn_gain_grad = jnp.sum(d_normed * unit_attn, axis=(0, 1))
    gain_grads = jnp.stack(
        [
            attn_gain_grad,
            ffn_gain_grad,
            jnp.pad(
                query_gain_grad.reshape(places.total, -1),
                ((0, 0), (0, shard_rows - query_gain.shape[0])),
            ).reshape(width),
        ],
        1,
    )
    gain_grads = jnp.pad(gain_grads, ((0, 0), (0, 128 - gain_grads.shape[1])))
    parts = jnp.concatenate([shared_grad.astype(BF), gain_grads.astype(BF)], 1)
    parts = parts.reshape(*places.dims, shard_rows, -1)
    core_parts = relative(parts, core_at, 3)
    query_up_grad = dot_tn(d_raw_all, latent_all).astype(BF)

    parts = sum_swaps(places, core_parts, CORE_DIM)
    half = parts.shape[-1] // 256 * 128
    first, second = parts[..., :half], parts[..., half:]
    first = sum_swaps(places, relative(first, pair_at, 2), PAIR_DIM)
    second = sum_swaps(places, relative(second, row_at, 1), ROW_DIM)
    first = sum_swaps(places, relative(first, row_at, 1), ROW_DIM)
    second = sum_swaps(places, relative(second, pair_at, 1), PAIR_DIM)
    parts = jnp.concatenate([first, second], -1)
    shared_grad = seq_sum(places, relative(parts, seq_at, 0))

    total = out_rows_grad[0].astype(F32)
    for a in out_row_away:
        total = total + a.astype(F32)
    out_grad = head_finish(total)
    total = sum_swaps(places, head_pairs(query_up_grad), PAIR_DIM)
    query_up_grad = head_finish(sum_swaps(places, head_row_parts(total), ROW_DIM)).T
    down_grad = row_total(down_total[0], down_came)
    gate_grad = row_total(gate_total[0], gate_came)
    up_grad = row_total(up_total[0], up_came)

    scaled = d_normed * attn_gain_f
    d_row = inv_attn * (
        scaled - unit_attn * jnp.mean(scaled * unit_attn, axis=-1, keepdims=True)
    )
    tokens_grad = (d_resid + d_row).astype(BF)
    layer_part = out_half[0] + out_pair_away.astype(F32)
    layer_rows = (resid + layer_part).astype(BF)

    return (
        layer_rows[:, None],
        tokens_grad[:, None],
        shared_grad[:, kv_end],
        shared_grad[:, :rank],
        shared_grad[: query_gain.shape[0], kv_end + 2],
        query_up_grad,
        shared_grad[:, rank : rank + HEAD_DIM],
        shared_grad[:, rank + HEAD_DIM : kv_end],
        out_grad,
        shared_grad[:, kv_end + 1],
        gate_grad.T,
        up_grad.T,
        down_grad,
    )


def solution(mesh):
    whole = P(AXES)
    rows = P(AXES, None)
    columns = P(None, AXES)
    packed = P(None, "dp", "seq", None)
    return jax.shard_map(
        body,
        mesh=mesh,
        in_specs=(
            packed,
            packed,
            P(None, "dp", None),
            P(None, "dp"),
            whole,
            rows,
            whole,
            columns,
            rows,
            rows,
            rows,
            whole,
            columns,
            columns,
            rows,
        ),
        out_specs=(
            packed,
            packed,
            whole,
            rows,
            whole,
            columns,
            rows,
            rows,
            rows,
            whole,
            columns,
            columns,
            rows,
        ),
        check_vma=False,
    )
```

```python
import itertools

import jax
import jax.numpy as jnp
from jax import lax
from jax.sharding import PartitionSpec as P

HEAD_DIM = 256
LONGEST = 512

EPSILON = 1e-05
THETA_BASE = 10000.0
NEG_FILL = -1e30

PAIR = 2
CORE = 2
SEQ_DIM, ROW_DIM, PAIR_DIM, CORE_DIM = 0, 1, 2, 3
AXES = ("seq", "dp")
SCORE_SCALE = HEAD_DIM ** (-0.5)

BF = jnp.bfloat16
F32 = jnp.float32


def inv_norm(values):
    return lax.rsqrt(jnp.mean(values * values, axis=-1, keepdims=True) + EPSILON)


def dot_nn(left_op, right_op):
    return jnp.dot(left_op, right_op, preferred_element_type=F32)


def dot_nt(left_op, right_op):
    return lax.dot_general(left_op, right_op, (((1,), (1,)), ((), ())), preferred_element_type=F32)


def dot_tn(left_op, right_op):
    return lax.dot_general(left_op, right_op, (((0,), (0,)), ((), ())), preferred_element_type=F32)


def angle_tables(positions, head_dim):
    half_dim = head_dim // 2
    frequency = jnp.power(THETA_BASE, -jnp.arange(half_dim, dtype=F32) * 2.0 / head_dim)
    angles = positions.astype(F32)[:, None] * frequency[None, :]
    cosine_tab = jnp.cos(angles)
    sine_tab = jnp.sin(angles)
    return (
        jnp.concatenate([cosine_tab, cosine_tab], -1),
        jnp.concatenate([sine_tab, sine_tab], -1),
    )


def rotary(values, cosine_tab, sine_tab):
    half_dim = values.shape[-1] // 2
    turned = jnp.concatenate([-values[..., half_dim:], values[..., :half_dim]], -1)
    return values * cosine_tab + turned * sine_tab


class Places:
    def __init__(self, seq_size, dp_size):
        self.dims = (seq_size, dp_size // (PAIR * CORE), PAIR, CORE)
        self.spots = list(itertools.product(*(range(n) for n in self.dims)))
        self.total = len(self.spots)

    def number(self, spot):
        flat = 0
        for size, at in zip(self.dims, spot):
            flat = flat * size + at
        return flat

    def fetch(self, value, dim, offset, wrap=True):
        if offset == 0:
            return value
        pairs = []
        for spot in self.spots:
            at = spot[dim] + offset
            if not wrap and not 0 <= at < self.dims[dim]:
                continue
            source = spot[:dim] + (at % self.dims[dim],) + spot[dim + 1 :]
            pairs.append((self.number(source), self.number(spot)))
        return lax.ppermute(value, AXES, pairs)

    def head_homes(self, head_blocks):
        pairs = []
        for block in range(self.total):
            head = block // head_blocks
            outer = (head // CORE) * head_blocks + block % head_blocks
            pairs.append((block, outer * CORE + head % CORE))
        return pairs


def absolute(chunks, index, dim):
    count = len(chunks)
    shape = list(chunks[0].shape)
    shape.insert(dim, count)
    turn = (lax.broadcasted_iota(jnp.int32, shape, dim) - index) % count
    value = jnp.expand_dims(chunks[0], dim)
    for k in range(1, count):
        value = jnp.where(turn == k, jnp.expand_dims(chunks[k], dim), value)
    return jnp.broadcast_to(value, shape)


def relative(values, index, dim):
    count = values.shape[dim]
    chunks = [lax.index_in_dim(values, i, dim, keepdims=False) for i in range(count)]
    placed = []
    for k in range(count):
        value = chunks[0]
        for position in range(1, count):
            value = jnp.where((index + k) % count == position, chunks[position], value)
        placed.append(value)
    return placed


def together(*values):
    return lax.optimization_barrier(values)


def seq_gather(places, block):
    return [places.fetch(block, SEQ_DIM, r) for r in range(places.dims[SEQ_DIM])]


def swap_gather(places, value, dim):
    return [places.fetch(value, dim, q) for q in range(places.dims[dim])]


def sum_swaps(places, parts, dim):
    total = parts[0].astype(F32)
    for q in range(1, len(parts)):
        total = total + places.fetch(parts[q].astype(BF), dim, -q).astype(F32)
    return total


def seq_sum(places, parts):
    total = parts[0].astype(F32)
    for r in range(1, len(parts)):
        total = total + places.fetch(parts[r].astype(BF), SEQ_DIM, -r).astype(F32)
    return total


def row_away(places, parts):
    return [places.fetch(parts[q], ROW_DIM, -1 - q) for q in range(len(parts))]


def row_total(own, came):
    total = own.astype(F32)
    for value in came:
        total = total + value.astype(F32)
    return total


def seq_away(places, total):
    return [places.fetch(total[r].astype(BF), SEQ_DIM, -r) for r in range(1, total.shape[0])]


def build_mask(query_pos, key_pos, lengths, pad_len, row_len):
    doc_ends = jnp.cumsum(lengths)
    query_seg = jnp.sum((query_pos[:, None] >= doc_ends[None, :]).astype(jnp.int32), 1)
    key_seg = jnp.sum((key_pos[:, None] >= doc_ends[None, :]).astype(jnp.int32), 1)
    valid_key = (key_pos < row_len - pad_len) & (key_pos >= 0)
    same_doc = (
        (query_seg[:, None] == key_seg[None, :])
        & (key_pos[None, :] <= query_pos[:, None])
        & valid_key[None, :]
    )
    return same_doc | (key_pos[None, :] == query_pos[:, None])


def attend(queries, keys, values, allowed):
    scores = jnp.einsum("bqhd,bkd->bhqk", queries, keys, preferred_element_type=F32) * SCORE_SCALE
    scores = jnp.where(allowed[:, None], scores, NEG_FILL)
    peak = jnp.max(scores, axis=-1, keepdims=True)
    expd = jnp.exp(scores - peak)
    total = jnp.sum(expd, axis=-1, keepdims=True)
    probs = expd / total
    mixture = jnp.einsum("bhqk,bkd->bqhd", probs.astype(BF), values, preferred_element_type=F32)
    return mixture.astype(BF), peak + jnp.log(total)


def attend_back(queries, keys, values, allowed, log_total, d_context):
    scores = jnp.einsum("bqhd,bkd->bhqk", queries, keys, preferred_element_type=F32) * SCORE_SCALE
    scores = jnp.where(allowed[:, None], scores, NEG_FILL)
    probs = jnp.exp(scores - log_total)
    d_probs = jnp.einsum("bqhd,bkd->bhqk", d_context, values, preferred_element_type=F32)
    d_values = jnp.einsum("bhqk,bqhd->bkd", probs.astype(BF), d_context, preferred_element_type=F32)
    d_scores = probs * (d_probs - jnp.sum(probs * d_probs, axis=-1, keepdims=True))
    d_scores = d_scores.astype(BF)
    d_queries = (
        jnp.einsum("bhqk,bkd->bqhd", d_scores, keys, preferred_element_type=F32) * SCORE_SCALE
    )
    d_keys = jnp.einsum("bhqk,bqhd->bkd", d_scores, queries, preferred_element_type=F32) * SCORE_SCALE
    return d_queries, d_keys, d_values


def body(
    tokens,
    cotangent,
    doc_lengths,
    pad_lengths,
    attn_gain,
    query_down,
    query_gain,
    query_up,
    key_weight,
    value_weight,
    out_weight,
    ffn_gain,
    gate_weight,
    up_weight,
    down_weight,
):
    places = Places(lax.axis_size("seq"), lax.axis_size("dp"))
    seq_n, row_n, pair_n, core_n = places.dims
    seq_at = lax.axis_index("seq")
    pair_at = (lax.axis_index("dp") // core_n) % pair_n
    row_at = lax.axis_index("dp") // (core_n * pair_n)
    core_at = lax.axis_index("dp") % core_n
    micro, _, local_len, width = tokens.shape
    row_len = local_len * seq_n
    rank = query_down.shape[1]
    head_blocks = HEAD_DIM // query_up.shape[1]
    hidden_block = gate_weight.shape[1]
    shard_rows = query_down.shape[0]

    head_wide = head_blocks > pair_n

    def head_rows(by_row):
        return absolute(by_row, row_at, 1) if head_wide else jnp.stack(by_row, 1)

    def both_cores(value):
        return jnp.stack([value, places.fetch(value, CORE_DIM, 1)], 1)

    gains = jnp.stack(
        [attn_gain, ffn_gain, jnp.pad(query_gain, (0, shard_rows - query_gain.shape[0]))], 1
    )
    gains = jnp.pad(gains, ((0, 0), (0, 128 - gains.shape[1])))
    shared = jnp.concatenate([query_down, key_weight, value_weight, gains], 1)
    homes = places.head_homes(head_blocks)
    up_home = lax.ppermute(query_up.T, AXES, homes)
    out_home = lax.ppermute(out_weight, AXES, homes)
    dys = cotangent[:, 0]
    shared_seq = seq_gather(places, shared)
    hs = tokens[:, 0].astype(F32)
    inv_attn = inv_norm(hs)
    lengths_both = both_cores(doc_lengths[:, 0])
    pads_both = both_cores(pad_lengths[:, 0])
    hidden_own = jnp.concatenate([gate_weight.T, up_weight.T, down_weight], 0)
    shared_seq, up_home, out_home, inv_attn, hidden_own = together(
        shared_seq, up_home, out_home, inv_attn, hidden_own
    )

    shared = absolute(shared_seq, seq_at, 0)
    shared_rows = swap_gather(places, shared, ROW_DIM)
    up_seq = seq_gather(places, up_home)
    out_near = [places.fetch(out_home, SEQ_DIM, r) for r in (1, -1)]
    shared_rows, up_seq, hidden_own = together(shared_rows, up_seq, hidden_own)

    shared = absolute(shared_rows, row_at, 1)
    shared_pairs = swap_gather(places, shared, PAIR_DIM)
    up_rows = swap_gather(places, jnp.stack(up_seq), ROW_DIM)
    shared_pairs, up_rows, out_near = together(shared_pairs, up_rows, out_near)

    shared = absolute(shared_pairs, pair_at, 2)
    shared = absolute(swap_gather(places, shared, CORE_DIM), core_at, 3)
    up_pairs = swap_gather(places, head_rows(up_rows), PAIR_DIM)
    out_seq = [out_home, out_near[0], places.fetch(out_near[0], SEQ_DIM, 1)]
    out_seq += [places.fetch(out_home, SEQ_DIM, r) for r in range(3, seq_n - 1)]
    out_seq.append(out_near[1])
    shared, out_seq = together(shared, out_seq)
    shared = shared.reshape(width, shared.shape[-1])

    out_rows = swap_gather(places, jnp.stack(out_seq), ROW_DIM)
    kv_end = rank + 2 * HEAD_DIM
    attn_gain_f = shared[:, kv_end].astype(F32)
    ffn_gain_f = shared[:, kv_end + 1].astype(F32)
    query_gain_f = (
        shared[:, kv_end + 2]
        .reshape(places.total, shard_rows)[:, : query_gain.shape[0]]
        .reshape(rank)
        .astype(F32)
    )
    unit_attn = hs * inv_attn
    normed = (unit_attn * attn_gain_f).astype(BF).reshape(micro * local_len, width)
    projected = dot_nn(normed, shared[:, :kv_end])

    def across_rows(block):
        return [places.fetch(block, ROW_DIM, q) for q in range(1, row_n)]

    latent = projected[:, :rank]
    inv_latent = inv_norm(latent)
    unit_latent = latent * inv_latent
    latent_normed = (unit_latent * query_gain_f).astype(BF)
    query_pos = seq_at * local_len + jnp.arange(local_len, dtype=jnp.int32)
    cosine, sine = angle_tables(query_pos, HEAD_DIM)
    keys_own = rotary(
        projected[:, rank : rank + HEAD_DIM].reshape(micro, local_len, HEAD_DIM), cosine, sine
    ).astype(BF)
    values_own = projected[:, rank + HEAD_DIM :].astype(BF).reshape(micro, local_len, HEAD_DIM)
    kv_own = jnp.concatenate([keys_own, values_own], -1)

    spans = min(seq_n, 1 + -(-(LONGEST - 1) // local_len))
    kv_row = [places.fetch(kv_own, SEQ_DIM, -k, wrap=False) for k in reversed(range(spans))]
    kv_row, out_heads, hidden_own = together(kv_row, head_rows(out_rows), hidden_own)
    out_pairs = swap_gather(places, out_heads, PAIR_DIM)
    hidden_ring = [hidden_own, places.fetch(hidden_own, SEQ_DIM, 1)]
    hidden_far = [across_rows(hidden_own)]
    kv_row = jnp.stack(kv_row, 1).reshape(micro, spans * local_len, 2 * HEAD_DIM)
    kv_both = both_cores(kv_row)
    latent_both = both_cores(latent_normed.reshape(micro, local_len, rank))
    key_pos = (seq_at - (spans - 1)) * local_len + jnp.arange(spans * local_len, dtype=jnp.int32)
    masks = jax.vmap(
        jax.vmap(lambda lengths, pad: build_mask(query_pos, key_pos, lengths, pad, row_len))
    )(lengths_both, pads_both)
    up_pairs, kv_both, latent_both, dys, hidden_ring, hidden_far = together(
        up_pairs, kv_both, latent_both, dys, hidden_ring, hidden_far
    )

    dy_pair = places.fetch(dys, PAIR_DIM, 1)
    query_up_t = absolute(up_pairs, pair_at, 2).reshape(-1, rank)
    heads = query_up_t.shape[0] // HEAD_DIM

    def group_cores(value, other):
        two = jnp.stack([value, other])
        return jnp.concatenate([two, places.fetch(two, CORE_DIM, 1)])


    def hidden_on(ring, far):
        return ring + [places.fetch(ring[-1], SEQ_DIM, 1)], far + [across_rows(ring[-1])]

    hidden_ring, hidden_far = hidden_on(hidden_ring, hidden_far)
    attended = []
    ffn_state = []
    ffn_rows = []
    for m in range(micro):
        keys_m, values_m = kv_both[m, :, :, :HEAD_DIM], kv_both[m, :, :, HEAD_DIM:]
        latent_m = latent_both[m].reshape(core_n * local_len, rank)
        raw = dot_nt(latent_m, query_up_t).reshape(core_n, local_len, heads, HEAD_DIM)
        queries = rotary(raw, cosine[:, None, :], sine[:, None, :]).astype(BF)
        context, log_total = attend(queries, keys_m, values_m, masks[m])
        context = context.reshape(core_n * local_len, heads * HEAD_DIM)
        if m == 0:
            context, out_pairs, hidden_ring, hidden_far = together(
                context, out_pairs, hidden_ring, hidden_far
            )
            out_full = absolute(out_pairs, pair_at, 2).reshape(-1, width)
        else:
            context, dy_pair, hidden_ring, hidden_far = together(
                context, dy_pair, hidden_ring, hidden_far
            )
        while len(hidden_ring) < seq_n and (m == 0 or m == micro - 1):
            hidden_ring, hidden_far = hidden_on(hidden_ring, hidden_far)
            if m == 0:
                break
        attended.append((queries, keys_m, values_m, log_total, context, latent_m))
        part = [
            dot_nn(context[k * local_len : (k + 1) * local_len], out_full) for k in range(core_n)
        ]
        resid = hs[m] + part[0] + places.fetch(part[1].astype(BF), CORE_DIM, 1).astype(F32)
        inv_ffn = inv_norm(resid)
        unit_ffn = resid * inv_ffn
        ffn_in = (unit_ffn * ffn_gain_f).astype(BF)
        ffn_in, kv_both, latent_both = together(ffn_in, kv_both, latent_both)
        ffn_state.append((resid, inv_ffn, unit_ffn))
        ffn_rows.append((ffn_in, places.fetch(ffn_in, PAIR_DIM, 1)))

    hidden_far.append(across_rows(hidden_ring[-1]))
    ffn_rows, hidden_far = together(ffn_rows, hidden_far)
    ffn_rows = group_cores(*(jnp.stack(a) for a in zip(*ffn_rows))).reshape(-1, width)
    dy_rows = group_cores(dys, dy_pair).reshape(-1, width)
    ffn_rows, dy_rows = together(ffn_rows, dy_rows)
    gate_t, up_t, down_t = (
        jnp.concatenate(
            [
                a[k * hidden_block : (k + 1) * hidden_block]
                for own, far in zip(hidden_ring, hidden_far)
                for a in [own] + far
            ],
            0,
        )
        for k in range(3)
    )

    def far_parts(grad):
        grad = grad.reshape(seq_n, row_n, hidden_block, width)
        return [grad[:, q] for q in range(1, row_n)]

    def own_parts(grad):
        return grad.reshape(seq_n, row_n, hidden_block, width)[:, 0]

    half_rows = pair_n * micro * local_len

    def group_scatter_core(part):
        away = part(slice(half_rows, None)).astype(BF)
        total = part(slice(0, half_rows)) + places.fetch(away, CORE_DIM, 1).astype(F32)
        return total.reshape(pair_n, micro, local_len, width)

    gate = dot_nt(ffn_rows, gate_t)
    up = dot_nt(ffn_rows, up_t)
    sig = jax.nn.sigmoid(gate)
    hidden = (gate * sig * up).astype(BF)
    d_hidden = dot_nt(dy_rows, down_t)
    d_gate = (d_hidden * up * (sig * (1.0 + gate * (1.0 - sig)))).astype(BF)
    d_up = (d_hidden * (gate * sig)).astype(BF)
    down_grad = dot_tn(hidden, dy_rows).astype(BF)
    d_gate, d_up, hidden, down_grad = together(d_gate, d_up, hidden, down_grad)

    down_came = row_away(places, far_parts(down_grad))
    d_ffn_half = group_scatter_core(
        lambda rows: dot_nn(d_gate[rows], gate_t) + dot_nn(d_up[rows], up_t)
    )
    d_ffn_out = d_ffn_half[1].astype(BF)
    d_ffn_half, d_ffn_out, hidden, d_gate, d_up = together(
        d_ffn_half, d_ffn_out, hidden, d_gate, d_up
    )
    d_ffn_away = places.fetch(d_ffn_out, PAIR_DIM, 1)
    gate_grad = dot_tn(d_gate, ffn_rows).astype(BF)
    up_grad = dot_tn(d_up, ffn_rows).astype(BF)
    out_half = group_scatter_core(lambda rows: dot_nn(hidden[rows], down_t))
    d_ffn_away, gate_grad, up_grad, out_half, down_came = together(
        d_ffn_away, gate_grad, up_grad, out_half, down_came
    )
    out_pair_away = places.fetch(out_half[1].astype(BF), PAIR_DIM, 1)
    gate_came = row_away(places, far_parts(gate_grad))
    down_total = row_total(own_parts(down_grad), down_came)
    down_came = seq_away(places, down_total)

    resid, inv_ffn, unit_ffn = (jnp.stack(a) for a in zip(*ffn_state))
    d_ffn_in = d_ffn_half[0] + d_ffn_away.astype(F32)
    ffn_gain_grad = jnp.sum(d_ffn_in * unit_ffn, axis=(0, 1))
    scaled = d_ffn_in * ffn_gain_f
    d_resid = dys.astype(F32) + inv_ffn * (
        scaled - unit_ffn * jnp.mean(scaled * unit_ffn, axis=-1, keepdims=True)
    )
    d_low_both = both_cores(d_resid.astype(BF))
    context_all = jnp.concatenate([a[4] for a in attended], 0)
    out_grad = dot_tn(context_all, d_low_both.reshape(-1, width)).astype(BF)
    out_grad, d_low_both, up_grad, out_pair_away, gate_came = together(
        out_grad, d_low_both, up_grad, out_pair_away, gate_came
    )
    up_came = row_away(places, far_parts(up_grad))
    gate_total = row_total(own_parts(gate_grad), gate_came)

    def head_pairs(grad):
        return relative(grad.reshape(seq_n, row_n, pair_n, -1, grad.shape[-1]), pair_at, 2)

    def head_row_parts(total):
        if head_wide:
            return relative(total, row_at, 1)
        return [total[:, q] for q in range(row_n)]

    def head_finish(total):
        back = [(dst, src) for src, dst in homes]
        total = seq_sum(places, [total[r] for r in range(seq_n)])
        return lax.ppermute(total.astype(BF), AXES, back).astype(F32)

    out_parts = head_pairs(out_grad)
    out_away = places.fetch(out_parts[1], PAIR_DIM, -1)
    d_latents = []
    d_kvs = []
    query_pairs = []
    for m in range(micro):
        queries, keys_m, values_m, log_total, context, latent_m = attended[m]
        d_low = d_low_both[m].reshape(-1, width)
        d_context = (
            dot_nt(d_low, out_full).astype(BF).reshape(core_n, local_len, heads, HEAD_DIM)
        )
        d_queries, d_keys, d_values = attend_back(
            queries, keys_m, values_m, masks[m], log_total, d_context
        )
        d_raw = rotary(d_queries, cosine[:, None, :], -sine[:, None, :]).astype(BF)
        d_raw = d_raw.reshape(core_n * local_len, heads * HEAD_DIM)
        part = dot_nn(d_raw, query_up_t).reshape(core_n, local_len, rank)
        d_latents.append(part[0] + places.fetch(part[1].astype(BF), CORE_DIM, 1).astype(F32))
        d_kv = jnp.concatenate([d_keys, d_values], -1)
        d_kv = d_kv[0] + places.fetch(d_kv[1].astype(BF), CORE_DIM, 1).astype(F32)
        d_kvs.append(d_kv.reshape(spans, local_len, 2 * HEAD_DIM))
        if m == 0:
            d_raw, d_latents, d_kvs, down_came, d_low_both = together(
                d_raw, d_latents, d_kvs, down_came, d_low_both
            )
            gate_came = seq_away(places, gate_total)
        query_pairs.append((d_raw, latent_m))
    d_raw_all, latent_all = (jnp.concatenate(a, 0) for a in zip(*query_pairs))
    d_latents, d_kvs, d_raw_all, out_away, gate_came, up_came = together(
        d_latents, d_kvs, d_raw_all, out_away, gate_came, up_came
    )
    up_total = row_total(own_parts(up_grad), up_came)

    up_came = seq_away(places, up_total)
    total = out_parts[0].astype(F32) + out_away.astype(F32)
    out_rows_grad = head_row_parts(total)
    out_row_away = [
        places.fetch(out_rows_grad[q].astype(BF), ROW_DIM, -q) for q in range(1, row_n)
    ]
    d_kv_all = jnp.stack(d_kvs)
    d_own = d_kv_all[:, spans - 1]
    for k in range(1, spans):
        d_own = d_own + places.fetch(
            d_kv_all[:, spans - 1 - k].astype(BF), SEQ_DIM, k, wrap=False
        ).astype(F32)
    d_latent_normed = jnp.concatenate(d_latents, 0)
    query_gain_grad = jnp.sum(d_latent_normed * unit_latent, axis=0)
    scaled = d_latent_normed * query_gain_f
    d_latent = (
        inv_latent * (scaled - unit_latent * jnp.mean(scaled * unit_latent, axis=-1, keepdims=True))
    ).astype(BF)
    d_key_raw = rotary(d_own[..., :HEAD_DIM], cosine, -sine).astype(BF)
    d_kv_low = jnp.concatenate([d_key_raw, d_own[..., HEAD_DIM:].astype(BF)], -1)
    d_kv_low = d_kv_low.reshape(micro * local_len, 2 * HEAD_DIM)
    d_both = jnp.concatenate([d_latent, d_kv_low], 1)
    shared_grad = dot_tn(normed, d_both)
    d_normed = dot_nt(d_both, shared[:, :kv_end]).reshape(micro, local_len, width)
    attn_gain_grad = jnp.sum(d_normed * unit_attn, axis=(0, 1))
    gain_grads = jnp.stack(
        [
            attn_gain_grad,
            ffn_gain_grad,
            jnp.pad(
                query_gain_grad.reshape(places.total, -1),
                ((0, 0), (0, shard_rows - query_gain.shape[0])),
            ).reshape(width),
        ],
        1,
    )
    gain_grads = jnp.pad(gain_grads, ((0, 0), (0, 128 - gain_grads.shape[1])))
    parts = jnp.concatenate([shared_grad.astype(BF), gain_grads.astype(BF)], 1)
    parts = parts.reshape(*places.dims, shard_rows, -1)
    core_parts = relative(parts, core_at, 3)
    query_up_grad = dot_tn(d_raw_all, latent_all).astype(BF)

    parts = sum_swaps(places, core_parts, CORE_DIM)
    half = parts.shape[-1] // 256 * 128
    first, second = parts[..., :half], parts[..., half:]
    first = sum_swaps(places, relative(first, pair_at, 2), PAIR_DIM)
    second = sum_swaps(places, relative(second, row_at, 1), ROW_DIM)
    first = sum_swaps(places, relative(first, row_at, 1), ROW_DIM)
    second = sum_swaps(places, relative(second, pair_at, 1), PAIR_DIM)
    parts = jnp.concatenate([first, second], -1)
    shared_grad = seq_sum(places, relative(parts, seq_at, 0))

    total = out_rows_grad[0].astype(F32)
    for a in out_row_away:
        total = total + a.astype(F32)
    out_grad = head_finish(total)
    total = sum_swaps(places, head_pairs(query_up_grad), PAIR_DIM)
    query_up_grad = head_finish(sum_swaps(places, head_row_parts(total), ROW_DIM)).T
    down_grad = row_total(down_total[0], down_came)
    gate_grad = row_total(gate_total[0], gate_came)
    up_grad = row_total(up_total[0], up_came)

    scaled = d_normed * attn_gain_f
    d_row = inv_attn * (
        scaled - unit_attn * jnp.mean(scaled * unit_attn, axis=-1, keepdims=True)
    )
    tokens_grad = (d_resid + d_row).astype(BF)
    layer_part = out_half[0] + out_pair_away.astype(F32)
    layer_rows = (resid + layer_part).astype(BF)

    return (
        layer_rows[:, None],
        tokens_grad[:, None],
        shared_grad[:, kv_end],
        shared_grad[:, :rank],
        shared_grad[: query_gain.shape[0], kv_end + 2],
        query_up_grad,
        shared_grad[:, rank : rank + HEAD_DIM],
        shared_grad[:, rank + HEAD_DIM : kv_end],
        out_grad,
        shared_grad[:, kv_end + 1],
        gate_grad.T,
        up_grad.T,
        down_grad,
    )


def solution(mesh):
    whole = P(AXES)
    rows = P(AXES, None)
    columns = P(None, AXES)
    packed = P(None, "dp", "seq", None)
    return jax.shard_map(
        body,
        mesh=mesh,
        in_specs=(
            packed,
            packed,
            P(None, "dp", None),
            P(None, "dp"),
            whole,
            rows,
            whole,
            columns,
            rows,
            rows,
            rows,
            whole,
            columns,
            columns,
            rows,
        ),
        out_specs=(
            packed,
            packed,
            whole,
            rows,
            whole,
            columns,
            rows,
            rows,
            rows,
            whole,
            columns,
            columns,
            rows,
        ),
        check_vma=False,
    )
```

```python
import itertools

import jax
import jax.numpy as jnp
from jax import lax
from jax.sharding import PartitionSpec as P

HEAD_DIM = 256
LONGEST = 512

EPSILON = 1e-05
THETA_BASE = 10000.0
NEG_FILL = -1e30

PAIR = 2
CORE = 2
SEQ_DIM, ROW_DIM, PAIR_DIM, CORE_DIM = 0, 1, 2, 3
AXES = ("seq", "dp")
SCORE_SCALE = HEAD_DIM ** (-0.5)

BF = jnp.bfloat16
F32 = jnp.float32


def inv_norm(values):
    return lax.rsqrt(jnp.mean(values * values, axis=-1, keepdims=True) + EPSILON)


def dot_nn(left_op, right_op):
    return jnp.dot(left_op, right_op, preferred_element_type=F32)


def dot_nt(left_op, right_op):
    return lax.dot_general(left_op, right_op, (((1,), (1,)), ((), ())), preferred_element_type=F32)


def dot_tn(left_op, right_op):
    return lax.dot_general(left_op, right_op, (((0,), (0,)), ((), ())), preferred_element_type=F32)


def angle_tables(positions, head_dim):
    half_dim = head_dim // 2
    frequency = jnp.power(THETA_BASE, -jnp.arange(half_dim, dtype=F32) * 2.0 / head_dim)
    angles = positions.astype(F32)[:, None] * frequency[None, :]
    cosine_tab = jnp.cos(angles)
    sine_tab = jnp.sin(angles)
    return (
        jnp.concatenate([cosine_tab, cosine_tab], -1),
        jnp.concatenate([sine_tab, sine_tab], -1),
    )


def rotary(values, cosine_tab, sine_tab):
    half_dim = values.shape[-1] // 2
    turned = jnp.concatenate([-values[..., half_dim:], values[..., :half_dim]], -1)
    return values * cosine_tab + turned * sine_tab


class Places:
    def __init__(self, seq_size, dp_size):
        self.dims = (seq_size, dp_size // (PAIR * CORE), PAIR, CORE)
        self.spots = list(itertools.product(*(range(n) for n in self.dims)))
        self.total = len(self.spots)

    def number(self, spot):
        flat = 0
        for size, at in zip(self.dims, spot):
            flat = flat * size + at
        return flat

    def fetch(self, value, dim, offset, wrap=True):
        if offset == 0:
            return value
        pairs = []
        for spot in self.spots:
            at = spot[dim] + offset
            if not wrap and not 0 <= at < self.dims[dim]:
                continue
            source = spot[:dim] + (at % self.dims[dim],) + spot[dim + 1 :]
            pairs.append((self.number(source), self.number(spot)))
        return lax.ppermute(value, AXES, pairs)

    def head_homes(self, head_blocks):
        pairs = []
        for block in range(self.total):
            head = block // head_blocks
            outer = (head // CORE) * head_blocks + block % head_blocks
            pairs.append((block, outer * CORE + head % CORE))
        return pairs


def absolute(chunks, index, dim):
    count = len(chunks)
    shape = list(chunks[0].shape)
    shape.insert(dim, count)
    turn = (lax.broadcasted_iota(jnp.int32, shape, dim) - index) % count
    value = jnp.expand_dims(chunks[0], dim)
    for k in range(1, count):
        value = jnp.where(turn == k, jnp.expand_dims(chunks[k], dim), value)
    return jnp.broadcast_to(value, shape)


def relative(values, index, dim):
    count = values.shape[dim]
    chunks = [lax.index_in_dim(values, i, dim, keepdims=False) for i in range(count)]
    placed = []
    for k in range(count):
        value = chunks[0]
        for position in range(1, count):
            value = jnp.where((index + k) % count == position, chunks[position], value)
        placed.append(value)
    return placed


def together(*values):
    return lax.optimization_barrier(values)


def seq_gather(places, block):
    return [places.fetch(block, SEQ_DIM, r) for r in range(places.dims[SEQ_DIM])]


def swap_gather(places, value, dim):
    return [places.fetch(value, dim, q) for q in range(places.dims[dim])]


def sum_swaps(places, parts, dim):
    total = parts[0].astype(F32)
    for q in range(1, len(parts)):
        total = total + places.fetch(parts[q].astype(BF), dim, -q).astype(F32)
    return total


def seq_sum(places, parts):
    total = parts[0].astype(F32)
    for r in range(1, len(parts)):
        total = total + places.fetch(parts[r].astype(BF), SEQ_DIM, -r).astype(F32)
    return total


def seq_relay_sum(places, parts):
    passed = places.fetch(parts[2].astype(BF), SEQ_DIM, -1)
    total = parts[0].astype(F32)
    for r in range(3, len(parts)):
        total = total + places.fetch(parts[r].astype(BF), SEQ_DIM, -r).astype(F32)
    onward = parts[1].astype(F32) + passed.astype(F32)
    return total + places.fetch(onward.astype(BF), SEQ_DIM, -1).astype(F32)


def row_away(places, parts):
    return [places.fetch(parts[q], ROW_DIM, -1 - q) for q in range(len(parts))]


def row_total(own, came):
    total = own.astype(F32)
    for value in came:
        total = total + value.astype(F32)
    return total


def seq_away(places, total):
    return [places.fetch(total[r].astype(BF), SEQ_DIM, -r) for r in range(1, total.shape[0])]


def build_mask(query_pos, key_pos, lengths, pad_len, row_len):
    doc_ends = jnp.cumsum(lengths)
    query_seg = jnp.sum((query_pos[:, None] >= doc_ends[None, :]).astype(jnp.int32), 1)
    key_seg = jnp.sum((key_pos[:, None] >= doc_ends[None, :]).astype(jnp.int32), 1)
    valid_key = (key_pos < row_len - pad_len) & (key_pos >= 0)
    same_doc = (
        (query_seg[:, None] == key_seg[None, :])
        & (key_pos[None, :] <= query_pos[:, None])
        & valid_key[None, :]
    )
    return same_doc | (key_pos[None, :] == query_pos[:, None])


def attend(queries, keys, values, allowed):
    scores = jnp.einsum("bqhd,bkd->bhqk", queries, keys, preferred_element_type=F32) * SCORE_SCALE
    scores = jnp.where(allowed[:, None], scores, NEG_FILL)
    peak = jnp.max(scores, axis=-1, keepdims=True)
    expd = jnp.exp(scores - peak)
    total = jnp.sum(expd, axis=-1, keepdims=True)
    probs = expd / total
    mixture = jnp.einsum("bhqk,bkd->bqhd", probs.astype(BF), values, preferred_element_type=F32)
    return mixture.astype(BF), peak + jnp.log(total)


def attend_back(queries, keys, values, allowed, log_total, d_context):
    scores = jnp.einsum("bqhd,bkd->bhqk", queries, keys, preferred_element_type=F32) * SCORE_SCALE
    scores = jnp.where(allowed[:, None], scores, NEG_FILL)
    probs = jnp.exp(scores - log_total)
    d_probs = jnp.einsum("bqhd,bkd->bhqk", d_context, values, preferred_element_type=F32)
    d_values = jnp.einsum("bhqk,bqhd->bkd", probs.astype(BF), d_context, preferred_element_type=F32)
    d_scores = probs * (d_probs - jnp.sum(probs * d_probs, axis=-1, keepdims=True))
    d_scores = d_scores.astype(BF)
    d_queries = (
        jnp.einsum("bhqk,bkd->bqhd", d_scores, keys, preferred_element_type=F32) * SCORE_SCALE
    )
    d_keys = jnp.einsum("bhqk,bqhd->bkd", d_scores, queries, preferred_element_type=F32) * SCORE_SCALE
    return d_queries, d_keys, d_values


def body(
    tokens,
    cotangent,
    doc_lengths,
    pad_lengths,
    attn_gain,
    query_down,
    query_gain,
    query_up,
    key_weight,
    value_weight,
    out_weight,
    ffn_gain,
    gate_weight,
    up_weight,
    down_weight,
):
    places = Places(lax.axis_size("seq"), lax.axis_size("dp"))
    seq_n, row_n, pair_n, core_n = places.dims
    seq_at = lax.axis_index("seq")
    pair_at = (lax.axis_index("dp") // core_n) % pair_n
    row_at = lax.axis_index("dp") // (core_n * pair_n)
    core_at = lax.axis_index("dp") % core_n
    micro, _, local_len, width = tokens.shape
    row_len = local_len * seq_n
    rank = query_down.shape[1]
    head_blocks = HEAD_DIM // query_up.shape[1]
    hidden_block = gate_weight.shape[1]
    shard_rows = query_down.shape[0]

    head_wide = head_blocks > pair_n

    def head_rows(by_row):
        return absolute(by_row, row_at, 1) if head_wide else jnp.stack(by_row, 1)

    def both_cores(value):
        return jnp.stack([value, places.fetch(value, CORE_DIM, 1)], 1)

    gains = jnp.stack(
        [attn_gain, ffn_gain, jnp.pad(query_gain, (0, shard_rows - query_gain.shape[0]))], 1
    )
    gains = jnp.pad(gains, ((0, 0), (0, 128 - gains.shape[1])))
    shared = jnp.concatenate([query_down, key_weight, value_weight, gains], 1)
    homes = places.head_homes(head_blocks)
    up_home = lax.ppermute(query_up.T, AXES, homes)
    out_home = lax.ppermute(out_weight, AXES, homes)
    dys = cotangent[:, 0]
    shared_seq = seq_gather(places, shared)
    hs = tokens[:, 0].astype(F32)
    inv_attn = inv_norm(hs)
    lengths_both = both_cores(doc_lengths[:, 0])
    pads_both = both_cores(pad_lengths[:, 0])
    hidden_own = jnp.concatenate([gate_weight.T, up_weight.T, down_weight], 0)
    shared_seq, up_home, out_home, inv_attn, hidden_own = together(
        shared_seq, up_home, out_home, inv_attn, hidden_own
    )

    shared = absolute(shared_seq, seq_at, 0)
    shared_rows = swap_gather(places, shared, ROW_DIM)
    up_seq = seq_gather(places, up_home)
    out_near = [places.fetch(out_home, SEQ_DIM, r) for r in (1, -1)]
    shared_rows, up_seq, hidden_own = together(shared_rows, up_seq, hidden_own)

    shared = absolute(shared_rows, row_at, 1)
    shared_pairs = swap_gather(places, shared, PAIR_DIM)
    up_rows = swap_gather(places, jnp.stack(up_seq), ROW_DIM)
    shared_pairs, up_rows, out_near = together(shared_pairs, up_rows, out_near)

    shared = absolute(shared_pairs, pair_at, 2)
    shared = absolute(swap_gather(places, shared, CORE_DIM), core_at, 3)
    up_pairs = swap_gather(places, head_rows(up_rows), PAIR_DIM)
    out_seq = [out_home, out_near[0], places.fetch(out_near[0], SEQ_DIM, 1)]
    out_seq += [places.fetch(out_home, SEQ_DIM, r) for r in range(3, seq_n - 1)]
    out_seq.append(out_near[1])
    shared, out_seq = together(shared, out_seq)
    shared = shared.reshape(width, shared.shape[-1])

    out_rows = swap_gather(places, jnp.stack(out_seq), ROW_DIM)
    kv_end = rank + 2 * HEAD_DIM
    attn_gain_f = shared[:, kv_end].astype(F32)
    ffn_gain_f = shared[:, kv_end + 1].astype(F32)
    query_gain_f = (
        shared[:, kv_end + 2]
        .reshape(places.total, shard_rows)[:, : query_gain.shape[0]]
        .reshape(rank)
        .astype(F32)
    )
    unit_attn = hs * inv_attn
    normed = (unit_attn * attn_gain_f).astype(BF).reshape(micro * local_len, width)
    projected = dot_nn(normed, shared[:, :kv_end])

    def across_rows(block):
        return [places.fetch(block, ROW_DIM, q) for q in range(1, row_n)]

    latent = projected[:, :rank]
    inv_latent = inv_norm(latent)
    unit_latent = latent * inv_latent
    latent_normed = (unit_latent * query_gain_f).astype(BF)
    query_pos = seq_at * local_len + jnp.arange(local_len, dtype=jnp.int32)
    cosine, sine = angle_tables(query_pos, HEAD_DIM)
    keys_own = rotary(
        projected[:, rank : rank + HEAD_DIM].reshape(micro, local_len, HEAD_DIM), cosine, sine
    ).astype(BF)
    values_own = projected[:, rank + HEAD_DIM :].astype(BF).reshape(micro, local_len, HEAD_DIM)
    kv_own = jnp.concatenate([keys_own, values_own], -1)

    spans = min(seq_n, 1 + -(-(LONGEST - 1) // local_len))
    kv_row = [places.fetch(kv_own, SEQ_DIM, -k, wrap=False) for k in reversed(range(spans))]
    kv_row, out_heads, hidden_own = together(kv_row, head_rows(out_rows), hidden_own)
    out_pairs = swap_gather(places, out_heads, PAIR_DIM)
    hidden_ring = [hidden_own, places.fetch(hidden_own, SEQ_DIM, 1)]
    hidden_far = [across_rows(hidden_own)]
    kv_row = jnp.stack(kv_row, 1).reshape(micro, spans * local_len, 2 * HEAD_DIM)
    kv_both = both_cores(kv_row)
    latent_both = both_cores(latent_normed.reshape(micro, local_len, rank))
    key_pos = (seq_at - (spans - 1)) * local_len + jnp.arange(spans * local_len, dtype=jnp.int32)
    masks = jax.vmap(
        jax.vmap(lambda lengths, pad: build_mask(query_pos, key_pos, lengths, pad, row_len))
    )(lengths_both, pads_both)
    up_pairs, kv_both, latent_both, dys, hidden_ring, hidden_far = together(
        up_pairs, kv_both, latent_both, dys, hidden_ring, hidden_far
    )

    dy_pair = places.fetch(dys, PAIR_DIM, 1)
    query_up_t = absolute(up_pairs, pair_at, 2).reshape(-1, rank)
    heads = query_up_t.shape[0] // HEAD_DIM

    def group_cores(value, other):
        two = jnp.stack([value, other])
        return jnp.concatenate([two, places.fetch(two, CORE_DIM, 1)])


    def hidden_on(ring, far):
        return ring + [places.fetch(ring[-1], SEQ_DIM, 1)], far + [across_rows(ring[-1])]

    hidden_ring, hidden_far = hidden_on(hidden_ring, hidden_far)
    attended = []
    ffn_state = []
    ffn_rows = []
    for m in range(micro):
        keys_m, values_m = kv_both[m, :, :, :HEAD_DIM], kv_both[m, :, :, HEAD_DIM:]
        latent_m = latent_both[m].reshape(core_n * local_len, rank)
        raw = dot_nt(latent_m, query_up_t).reshape(core_n, local_len, heads, HEAD_DIM)
        queries = rotary(raw, cosine[:, None, :], sine[:, None, :]).astype(BF)
        context, log_total = attend(queries, keys_m, values_m, masks[m])
        context = context.reshape(core_n * local_len, heads * HEAD_DIM)
        if m == 0:
            context, out_pairs, hidden_ring, hidden_far = together(
                context, out_pairs, hidden_ring, hidden_far
            )
            out_full = absolute(out_pairs, pair_at, 2).reshape(-1, width)
        else:
            context, dy_pair, hidden_ring, hidden_far = together(
                context, dy_pair, hidden_ring, hidden_far
            )
        while len(hidden_ring) < seq_n and (m == 0 or m == micro - 1):
            hidden_ring, hidden_far = hidden_on(hidden_ring, hidden_far)
            if m == 0:
                break
        attended.append((queries, keys_m, values_m, log_total, context, latent_m))
        part = [
            dot_nn(context[k * local_len : (k + 1) * local_len], out_full) for k in range(core_n)
        ]
        resid = hs[m] + part[0] + places.fetch(part[1].astype(BF), CORE_DIM, 1).astype(F32)
        inv_ffn = inv_norm(resid)
        unit_ffn = resid * inv_ffn
        ffn_in = (unit_ffn * ffn_gain_f).astype(BF)
        ffn_in, kv_both, latent_both = together(ffn_in, kv_both, latent_both)
        ffn_state.append((resid, inv_ffn, unit_ffn))
        ffn_rows.append((ffn_in, places.fetch(ffn_in, PAIR_DIM, 1)))

    hidden_far.append(across_rows(hidden_ring[-1]))
    ffn_rows, hidden_far = together(ffn_rows, hidden_far)
    ffn_rows = group_cores(*(jnp.stack(a) for a in zip(*ffn_rows))).reshape(-1, width)
    dy_rows = group_cores(dys, dy_pair).reshape(-1, width)
    ffn_rows, dy_rows = together(ffn_rows, dy_rows)
    gate_t, up_t, down_t = (
        jnp.concatenate(
            [
                a[k * hidden_block : (k + 1) * hidden_block]
                for own, far in zip(hidden_ring, hidden_far)
                for a in [own] + far
            ],
            0,
        )
        for k in range(3)
    )

    def far_parts(grad):
        grad = grad.reshape(seq_n, row_n, hidden_block, width)
        return [grad[:, q] for q in range(1, row_n)]

    def own_parts(grad):
        return grad.reshape(seq_n, row_n, hidden_block, width)[:, 0]

    half_rows = pair_n * micro * local_len

    def group_scatter_core(part):
        away = part(slice(half_rows, None)).astype(BF)
        total = part(slice(0, half_rows)) + places.fetch(away, CORE_DIM, 1).astype(F32)
        return total.reshape(pair_n, micro, local_len, width)

    gate = dot_nt(ffn_rows, gate_t)
    up = dot_nt(ffn_rows, up_t)
    sig = jax.nn.sigmoid(gate)
    hidden = (gate * sig * up).astype(BF)
    d_hidden = dot_nt(dy_rows, down_t)
    d_gate = (d_hidden * up * (sig * (1.0 + gate * (1.0 - sig)))).astype(BF)
    d_up = (d_hidden * (gate * sig)).astype(BF)
    down_grad = dot_tn(hidden, dy_rows).astype(BF)
    d_gate, d_up, hidden, down_grad = together(d_gate, d_up, hidden, down_grad)

    down_came = row_away(places, far_parts(down_grad))
    d_ffn_half = group_scatter_core(
        lambda rows: dot_nn(d_gate[rows], gate_t) + dot_nn(d_up[rows], up_t)
    )
    d_ffn_out = d_ffn_half[1].astype(BF)
    d_ffn_half, d_ffn_out, hidden, d_gate, d_up = together(
        d_ffn_half, d_ffn_out, hidden, d_gate, d_up
    )
    d_ffn_away = places.fetch(d_ffn_out, PAIR_DIM, 1)
    gate_grad = dot_tn(d_gate, ffn_rows).astype(BF)
    up_grad = dot_tn(d_up, ffn_rows).astype(BF)
    out_half = group_scatter_core(lambda rows: dot_nn(hidden[rows], down_t))
    d_ffn_away, gate_grad, up_grad, out_half, down_came = together(
        d_ffn_away, gate_grad, up_grad, out_half, down_came
    )
    out_pair_away = places.fetch(out_half[1].astype(BF), PAIR_DIM, 1)
    gate_came = row_away(places, far_parts(gate_grad))
    down_total = row_total(own_parts(down_grad), down_came)
    down_came = seq_away(places, down_total)

    resid, inv_ffn, unit_ffn = (jnp.stack(a) for a in zip(*ffn_state))
    d_ffn_in = d_ffn_half[0] + d_ffn_away.astype(F32)
    ffn_gain_grad = jnp.sum(d_ffn_in * unit_ffn, axis=(0, 1))
    scaled = d_ffn_in * ffn_gain_f
    d_resid = dys.astype(F32) + inv_ffn * (
        scaled - unit_ffn * jnp.mean(scaled * unit_ffn, axis=-1, keepdims=True)
    )
    d_low_both = both_cores(d_resid.astype(BF))
    context_all = jnp.concatenate([a[4] for a in attended], 0)
    out_grad = dot_tn(context_all, d_low_both.reshape(-1, width)).astype(BF)
    out_grad, d_low_both, up_grad, out_pair_away, gate_came = together(
        out_grad, d_low_both, up_grad, out_pair_away, gate_came
    )
    up_came = row_away(places, far_parts(up_grad))
    gate_total = row_total(own_parts(gate_grad), gate_came)

    def head_pairs(grad):
        return relative(grad.reshape(seq_n, row_n, pair_n, -1, grad.shape[-1]), pair_at, 2)

    def head_row_parts(total):
        if head_wide:
            return relative(total, row_at, 1)
        return [total[:, q] for q in range(row_n)]

    def head_finish(total):
        back = [(dst, src) for src, dst in homes]
        total = seq_relay_sum(places, [total[r] for r in range(seq_n)])
        return lax.ppermute(total.astype(BF), AXES, back).astype(F32)

    out_parts = head_pairs(out_grad)
    out_away = places.fetch(out_parts[1], PAIR_DIM, -1)
    d_latents = []
    d_kvs = []
    query_pairs = []
    for m in range(micro):
        queries, keys_m, values_m, log_total, context, latent_m = attended[m]
        d_low = d_low_both[m].reshape(-1, width)
        d_context = (
            dot_nt(d_low, out_full).astype(BF).reshape(core_n, local_len, heads, HEAD_DIM)
        )
        d_queries, d_keys, d_values = attend_back(
            queries, keys_m, values_m, masks[m], log_total, d_context
        )
        d_raw = rotary(d_queries, cosine[:, None, :], -sine[:, None, :]).astype(BF)
        d_raw = d_raw.reshape(core_n * local_len, heads * HEAD_DIM)
        part = dot_nn(d_raw, query_up_t).reshape(core_n, local_len, rank)
        d_latents.append(part[0] + places.fetch(part[1].astype(BF), CORE_DIM, 1).astype(F32))
        d_kv = jnp.concatenate([d_keys, d_values], -1)
        d_kv = d_kv[0] + places.fetch(d_kv[1].astype(BF), CORE_DIM, 1).astype(F32)
        d_kvs.append(d_kv.reshape(spans, local_len, 2 * HEAD_DIM))
        if m == 0:
            d_raw, d_latents, d_kvs, down_came, d_low_both = together(
                d_raw, d_latents, d_kvs, down_came, d_low_both
            )
            gate_came = seq_away(places, gate_total)
        query_pairs.append((d_raw, latent_m))
    d_raw_all, latent_all = (jnp.concatenate(a, 0) for a in zip(*query_pairs))
    d_latents, d_kvs, d_raw_all, out_away, gate_came, up_came = together(
        d_latents, d_kvs, d_raw_all, out_away, gate_came, up_came
    )
    up_total = row_total(own_parts(up_grad), up_came)

    up_grad = seq_relay_sum(places, [up_total[r] for r in range(seq_n)])
    total = out_parts[0].astype(F32) + out_away.astype(F32)
    out_rows_grad = head_row_parts(total)
    out_row_away = [
        places.fetch(out_rows_grad[q].astype(BF), ROW_DIM, -q) for q in range(1, row_n)
    ]
    d_kv_all = jnp.stack(d_kvs)
    d_own = d_kv_all[:, spans - 1]
    for k in range(1, spans):
        d_own = d_own + places.fetch(
            d_kv_all[:, spans - 1 - k].astype(BF), SEQ_DIM, k, wrap=False
        ).astype(F32)
    d_latent_normed = jnp.concatenate(d_latents, 0)
    query_gain_grad = jnp.sum(d_latent_normed * unit_latent, axis=0)
    scaled = d_latent_normed * query_gain_f
    d_latent = (
        inv_latent * (scaled - unit_latent * jnp.mean(scaled * unit_latent, axis=-1, keepdims=True))
    ).astype(BF)
    d_key_raw = rotary(d_own[..., :HEAD_DIM], cosine, -sine).astype(BF)
    d_kv_low = jnp.concatenate([d_key_raw, d_own[..., HEAD_DIM:].astype(BF)], -1)
    d_kv_low = d_kv_low.reshape(micro * local_len, 2 * HEAD_DIM)
    d_both = jnp.concatenate([d_latent, d_kv_low], 1)
    shared_grad = dot_tn(normed, d_both)
    d_normed = dot_nt(d_both, shared[:, :kv_end]).reshape(micro, local_len, width)
    attn_gain_grad = jnp.sum(d_normed * unit_attn, axis=(0, 1))
    gain_grads = jnp.stack(
        [
            attn_gain_grad,
            ffn_gain_grad,
            jnp.pad(
                query_gain_grad.reshape(places.total, -1),
                ((0, 0), (0, shard_rows - query_gain.shape[0])),
            ).reshape(width),
        ],
        1,
    )
    gain_grads = jnp.pad(gain_grads, ((0, 0), (0, 128 - gain_grads.shape[1])))
    parts = jnp.concatenate([shared_grad.astype(BF), gain_grads.astype(BF)], 1)
    parts = parts.reshape(*places.dims, shard_rows, -1)
    core_parts = relative(parts, core_at, 3)
    query_up_grad = dot_tn(d_raw_all, latent_all).astype(BF)

    parts = sum_swaps(places, core_parts, CORE_DIM)
    half = parts.shape[-1] // 256 * 128
    first, second = parts[..., :half], parts[..., half:]
    first = sum_swaps(places, relative(first, pair_at, 2), PAIR_DIM)
    second = sum_swaps(places, relative(second, row_at, 1), ROW_DIM)
    first = sum_swaps(places, relative(first, row_at, 1), ROW_DIM)
    second = sum_swaps(places, relative(second, pair_at, 1), PAIR_DIM)
    parts = jnp.concatenate([first, second], -1)
    shared_grad = seq_sum(places, relative(parts, seq_at, 0))

    total = out_rows_grad[0].astype(F32)
    for a in out_row_away:
        total = total + a.astype(F32)
    out_grad = head_finish(total)
    total = sum_swaps(places, head_pairs(query_up_grad), PAIR_DIM)
    query_up_grad = head_finish(sum_swaps(places, head_row_parts(total), ROW_DIM)).T
    down_grad = row_total(down_total[0], down_came)
    gate_grad = row_total(gate_total[0], gate_came)

    scaled = d_normed * attn_gain_f
    d_row = inv_attn * (
        scaled - unit_attn * jnp.mean(scaled * unit_attn, axis=-1, keepdims=True)
    )
    tokens_grad = (d_resid + d_row).astype(BF)
    layer_part = out_half[0] + out_pair_away.astype(F32)
    layer_rows = (resid + layer_part).astype(BF)

    return (
        layer_rows[:, None],
        tokens_grad[:, None],
        shared_grad[:, kv_end],
        shared_grad[:, :rank],
        shared_grad[: query_gain.shape[0], kv_end + 2],
        query_up_grad,
        shared_grad[:, rank : rank + HEAD_DIM],
        shared_grad[:, rank + HEAD_DIM : kv_end],
        out_grad,
        shared_grad[:, kv_end + 1],
        gate_grad.T,
        up_grad.T,
        down_grad,
    )


def solution(mesh):
    whole = P(AXES)
    rows = P(AXES, None)
    columns = P(None, AXES)
    packed = P(None, "dp", "seq", None)
    return jax.shard_map(
        body,
        mesh=mesh,
        in_specs=(
            packed,
            packed,
            P(None, "dp", None),
            P(None, "dp"),
            whole,
            rows,
            whole,
            columns,
            rows,
            rows,
            rows,
            whole,
            columns,
            columns,
            rows,
        ),
        out_specs=(
            packed,
            packed,
            whole,
            rows,
            whole,
            columns,
            rows,
            rows,
            rows,
            whole,
            columns,
            columns,
            rows,
        ),
        check_vma=False,
    )
```
